32 devices in a mesh: hi: 4 (over x, core), lo: 8 (over z, y).
Axes of the slice: x: 2, y: 2, z: 4, core: 2. Of those that a mesh axis runs over, the one named last changes fastest.
Arguments:
- current: float32 [131072, 256], P(('hi', 'lo')), may hold values from -130 to 130
- signs: int32 [131072], P(('hi', 'lo')), may hold values from -1 to 1, as said below
- sample_rows: int32 [512], P(('hi', 'lo')), may hold values from 0 to 4095
- sample_owner: int32 [512, 1], P(('hi', 'lo')), may hold values from 0 to 7; in each aligned block of 16 rows (0 to 15, 16 to 31, ...) at most 2 rows name the same one
Outputs:
- sketch: float32 [4, 8, 8, 2, 256], P('hi', 'lo')
- r_factor: float32 [256, 256], replicated
- precond: float32 [131072, 256], P(('hi', 'lo'))
The draws below stay inside these ranges and needn't reach their ends.
Inputs may be any that keep to these rules, and one draw needn't show every extreme that they name: `signs`: each entry is -1 or 1. `sample_owner`: among the 16 samples of one device no owner is named more than 2 times, and in every draw some device names some owner exactly 2 times.
All inputs are finite; a program needn't handle non-finite values.
Results may differ from the reference program's by a relative error of at most 0.000098.
Values sent between devices are 32-bit elements; how exact they have to be, the bound alone decides.
A program may use at most 64 MiB of HBM per device.

```python
import math
import jax
import jax.numpy as jnp
import numpy as np
from jax import lax

P_SIZE = 256
ROWS_DEV = 4096
SAMP_DEV = 16
MOST = 2
TOTAL_ROWS = 131072
SAMPLES = 512
N_HI = 4
N_LO = 8


def draw_current(key, part):
    key_vals, key_rows, key_cols = jax.random.split(key, 3)
    row_scale = jnp.exp(jax.random.uniform(key_rows, (TOTAL_ROWS, 1), jnp.float32, -1.15, 1.15))
    col_scale = jnp.exp(jax.random.uniform(key_cols, (1, P_SIZE), jnp.float32, -1.15, 1.15))
    ramp_rows = 1.0 + 2.0 * jnp.arange(TOTAL_ROWS, dtype=jnp.float32)[:, None] / (TOTAL_ROWS - 1)
    values_base = jnp.clip(jax.random.normal(key_vals, (TOTAL_ROWS, P_SIZE), jnp.float32), -4.0, 4.0)
    return values_base * row_scale * ramp_rows * col_scale


def draw_signs(key, part):
    return (2 * jax.random.randint(key, (TOTAL_ROWS,), 0, 2) - 1).astype(jnp.int32)


def place_ends(drawn, stream_key, least, top_value):
    dims = drawn.shape
    spot = [jax.random.randint(jax.random.fold_in(stream_key, axis), (), 0, dims[axis]) for axis in range(len(dims))]
    drawn = drawn.at[tuple(spot)].set(least)
    longest = dims.index(max(dims))
    spot[longest] = (spot[longest] + 1) % dims[longest]
    return drawn.at[tuple(spot)].set(top_value)


def assign_block(stream_key, own, number, rows, count, top, bound, lean):
    sequence = jax.random.permutation(stream_key, count)
    packed, usual = shares(count, rows * top, bound, lean, True), shares(count, rows * top, bound, lean, False)
    places = jnp.arange(count)

    def named(tallies, turn):
        used = int((tallies > 0).sum())
        fixed = max(1, used // 4)
        shifted = fixed + (places - fixed + turn * (used - fixed)) % max(1, count - fixed)
        return jnp.zeros((count,), jnp.int32).at[sequence[jnp.where(places < fixed, places, shifted)]].set(jnp.asarray(tallies, jnp.int32))

    tallies = jnp.where(number % 4 == 0, named(packed, number // 4), named(usual, number - number // 4 - 1))
    mixed = jax.random.permutation(jax.random.fold_in(own, 3), count)
    giver, receiver = mixed[0:count // 2 * 2:2], mixed[1:count // 2 * 2:2]
    slack = jnp.minimum(tallies[giver] - 1, bound - tallies[receiver]) // 2
    slack = jnp.where((giver == sequence[0]) | (receiver == sequence[0]) | (tallies[receiver] == 0), 0, jnp.maximum(slack, 0))
    shifted = jax.random.randint(jax.random.fold_in(own, 4), (count // 2,), 0, 1 << 20) % (slack + 1)
    tallies = tallies.at[giver].add(-shifted).at[receiver].add(shifted)
    labels = jnp.searchsorted(jnp.cumsum(tallies), jnp.arange(rows * top), side="right").astype(jnp.int32)
    table = labels.reshape(top, rows).T
    table = table[jax.random.permutation(jax.random.fold_in(own, 1), rows)]
    turn = jax.random.randint(jax.random.fold_in(own, 2), (rows, 1), 0, top)
    return jnp.take_along_axis(table, (jnp.arange(top)[None, :] + turn) % top, axis=1)


def shares(count, total, most, slope, full):
    portions = [(1 << 20) // math.isqrt(rank ** slope) + 1 for rank in range(1, count + 1)]
    largest = most if full else min(most, max(-(-total // count), total * portions[0] // sum(portions)))
    least = 1 if total - largest >= count - 1 else 0
    holding, rest = [largest] + [least] * (count - 1), total - largest - least * (count - 1)
    while rest > 0:
        candidates = [i for i in range(1, count) if holding[i] < largest] or [i for i in range(1, count) if holding[i] < most]
        mass, left = sum([portions[i] for i in candidates]), rest
        for i in candidates:
            more = min(most - holding[i], max(1, left * portions[i] // mass), rest)
            holding[i] = holding[i] + more
            rest = rest - more
    return np.array(holding)


def setup_inputs(seed: int = 0) -> dict:
    keys = jax.random.split(jax.random.key(seed), 5)
    current = draw_current(jax.random.fold_in(keys[4], 71), 0)
    signs = draw_signs(jax.random.fold_in(keys[4], 71), 0)
    sample_rows = place_ends(jax.random.randint(keys[2], (SAMPLES,), 0, ROWS_DEV), jax.random.fold_in(keys[2], 1), 0, ROWS_DEV - 1).astype(jnp.int32)
    sample_owner_keys = jax.random.split(jax.random.fold_in(keys[3], 1), SAMPLES // SAMP_DEV)
    sample_owner_turns = jax.random.permutation(jax.random.fold_in(keys[3], 3), SAMPLES // SAMP_DEV)
    sample_owner = jax.vmap(lambda own, number: assign_block(jax.random.fold_in(keys[3], 2), own, number, SAMP_DEV, N_LO, 1, MOST, 2))(sample_owner_keys, sample_owner_turns).reshape((SAMPLES, 1))
    return dict(current=current, signs=signs, sample_rows=sample_rows, sample_owner=sample_owner)


HIGHEST = lax.Precision.HIGHEST

def sylvester(order_size):
    hadamard_table = jnp.ones((1, 1), jnp.float32)
    base_pair = jnp.array([[1.0, 1.0], [1.0, -1.0]], jnp.float32)
    while hadamard_table.shape[0] < order_size:
        hadamard_table = jnp.kron(hadamard_table, base_pair)
    return hadamard_table

def split_order(order_size):
    leading = 2 ** ((order_size.bit_length() - 1) // 2)
    return (leading, order_size // leading)

def reference(current, signs, sample_rows, sample_owner):
    devices = N_HI * N_LO
    signed = current * signs.astype(jnp.float32)[:, None]
    leading, second = split_order(ROWS_DEV)
    shaped = signed.reshape(devices, leading, second, P_SIZE)
    shaped = jnp.einsum('ab,gbcp->gacp', sylvester(leading), shaped, precision=HIGHEST)
    shaped = jnp.einsum('cd,gadp->gacp', sylvester(second), shaped, precision=HIGHEST)
    shaped = shaped.reshape(devices, ROWS_DEV, P_SIZE)
    crossed = jnp.einsum('gh,hrp->grp', sylvester(devices), shaped, precision=HIGHEST)
    flat_rows = crossed.reshape(TOTAL_ROWS, P_SIZE)
    device_of = jnp.arange(SAMPLES, dtype=jnp.int32) // SAMP_DEV
    global_rows = (device_of * ROWS_DEV + sample_rows).astype(jnp.int32)
    picked = jnp.take(flat_rows, global_rows, axis=0) * (1.0 / math.sqrt(TOTAL_ROWS))
    owner_ids = sample_owner[:, 0]
    owner_hot = (owner_ids[:, None] == jnp.arange(N_LO, dtype=jnp.int32)[None, :]).astype(jnp.int32)
    hot_device = owner_hot.reshape(devices, SAMP_DEV, N_LO)
    before = jnp.cumsum(hot_device, axis=1) - hot_device
    slot_ids = lax.optimization_barrier(jnp.sum(before * hot_device, axis=2)).reshape(SAMPLES)
    sketch = jnp.zeros((N_HI, N_LO, N_LO, MOST, P_SIZE), jnp.float32)
    sketch = sketch.at[device_of // N_LO, owner_ids, device_of % N_LO, slot_ids].set(picked)
    gram_total = jnp.dot(picked.T, picked, precision=HIGHEST) * (1.0 / SAMPLES)
    lower_factor = jnp.linalg.cholesky(gram_total)
    precond = lax.linalg.triangular_solve(lower_factor, current, left_side=False, lower=True, transpose_a=True)
    return (sketch, lower_factor.T, precond)
```

```python
import functools
import math

import jax
import jax.numpy as jnp
from jax import lax
from jax.experimental import pallas as pl
from jax.experimental.pallas import tpu as pltpu
from jax.sharding import PartitionSpec as P

MOST = 2
LANES = 128
BLOCK = 64
TILE = 256
EARLY = 8
VMEM_LIMIT = 61 * 2 ** 20
MESH = pl.DeviceIdType.MESH
HIGHEST = lax.Precision.HIGHEST
F32 = jnp.float32
BF16 = jnp.bfloat16


def bits_of(size):
    return size.bit_length() - 1


def parity(value, top):
    shift = 1
    while shift * 2 < top:
        shift *= 2
    while shift >= 1:
        value = value ^ (value >> shift)
        shift //= 2
    return value & 1


def mix_kernel(nh, nl, count, rows_hbm, owner_hbm, signs_hbm, current_ref, gram_ref, sketch_ref,
               rows_ref, owner_ref, signs_ref, note_ref, notes, places, xbuf, ybuf, share, pair_in, mid_in, far_in, gathered,
               small_sem, load_sem, place_sem, nsend, nrecv, psend, precv, msend, mrecv, fsend, frecv,
               gfsend, gfrecv, gmsend, gmrecv, gpsend, gprecv):
    hi, lo = lax.axis_index("hi"), lax.axis_index("lo")
    bh, bl = bits_of(nh), bits_of(nl)
    devices = nh * nl
    rows, width = current_ref.shape
    total = devices * count
    loads = rows // TILE
    fars, mids = nl // 2, nh
    far_rows, mid_rows, half = count, count * fars, count * fars * mids

    def masks(p):
        return (((p >> bl) & (nh // 2 - 1)) << 1 | (p >> (bl + bh - 1)),
                ((p << 1) & (nl - 1)) | ((p >> (bl - 1)) & 1))

    def peer(p):
        mask_hi, mask_lo = masks(p)
        return (hi ^ mask_hi, lo ^ mask_lo)

    def load(c):
        at = pl.ds(c * TILE, TILE)
        return pltpu.make_async_copy(current_ref.at[at, :], xbuf.at[at, :], load_sem.at[c])

    small = [pltpu.make_async_copy(source, target, small_sem.at[k])
             for k, (source, target) in enumerate(
                 ((rows_hbm, rows_ref), (owner_hbm, owner_ref), (signs_hbm, signs_ref)))]
    for copy in small:
        copy.start()
    barrier = pltpu.get_barrier_semaphore()
    for p in range(1, devices):
        pl.semaphore_signal(barrier, inc=1, device_id=peer(p), device_id_type=MESH)
    for c in range(loads):
        load(c).start()
    for copy in small:
        copy.wait()
    note_ref[...] = jnp.zeros_like(note_ref)
    note_ref[:, 0:count] = rows_ref[...]
    note_ref[:, count:2 * count] = owner_ref[...]

    up = lax.broadcasted_iota(jnp.int32, (TILE, TILE), 0)
    across = lax.broadcasted_iota(jnp.int32, (TILE, TILE), 1)
    table = (1 - 2 * parity(up & across, TILE)).astype(F32).astype(BF16)

    def transform(c):
        load(c).wait()
        at = slice(c * TILE, (c + 1) * TILE)
        lanes = TILE // LANES
        sign = jnp.concatenate([signs_ref[c * lanes + k:c * lanes + k + 1, :] for k in range(lanes)], axis=1)
        signed = table * sign.astype(F32).astype(BF16)
        x = xbuf[at, :]
        top = x.astype(BF16)
        rest = (x - top.astype(F32)).astype(BF16)
        ybuf[at, :] = (jnp.dot(signed, top, preferred_element_type=F32)
                       + jnp.dot(signed, rest, preferred_element_type=F32))

    early = loads * EARLY // 16
    for c in range(early):
        transform(c)
    pl.semaphore_wait(barrier, devices - 1)

    def note(p):
        return pltpu.make_async_remote_copy(
            src_ref=note_ref, dst_ref=notes.at[pl.ds(p, 1), :],
            send_sem=nsend.at[p], recv_sem=nrecv.at[p],
            device_id=peer(p), device_id_type=MESH)

    for p in range(1, devices):
        note(p).start()
    notes[0:1, :] = note_ref[...]
    for c in range(early, loads):
        transform(c)

    @pl.loop(0, TILE // 8)
    def _(r):
        first = pl.multiple_of(r * 8, 8)
        block = [ybuf[pl.ds(first + c * TILE, 8), :] for c in range(loads)]
        step = 1
        while step < loads:
            block = [block[c] + block[c + step] if not c & step else block[c - step] - block[c]
                     for c in range(loads)]
            step *= 2
        for c in range(loads):
            ybuf[pl.ds(first + c * TILE, 8), :] = block[c]

    for p in range(1, devices):
        note(p).wait_recv()
    spread = pltpu.make_async_copy(notes, places, place_sem)
    spread.start()
    spread.wait()

    def pick(first, size):
        @pl.loop(first // count, (first + size) // count)
        def _(p):
            mask_hi, mask_lo = masks(p)
            odd = parity(((hi & ~mask_hi) << bl) | (lo & ~mask_lo), devices)
            flip = (1 - 2 * odd).astype(F32)
            base = pl.multiple_of(p * count, count)
            for i in range(count):
                share[pl.ds(base + i, 1), :] = ybuf[pl.ds(places[p, i], 1), :] * flip

    def remote(source, target, send, recv, p):
        return pltpu.make_async_remote_copy(src_ref=source, dst_ref=target, send_sem=send, recv_sem=recv,
                                            device_id=peer(p), device_id_type=MESH)

    pair = devices // 2

    def pair_sum(q):
        return remote(share.at[pl.ds(half + q * mid_rows, mid_rows), :], pair_in.at[pl.ds(q * mid_rows, mid_rows), :],
                      psend.at[q], precv.at[q], pair)

    def mid_sum(q):
        return remote(share.at[pl.ds(q * mid_rows, mid_rows), :], mid_in.at[pl.ds(q * mid_rows, mid_rows), :],
                      msend.at[q], mrecv.at[q], q * fars)

    def far_sum(q):
        return remote(share.at[pl.ds(q * far_rows, far_rows), :], far_in.at[pl.ds(q * far_rows, far_rows), :],
                      fsend.at[q], frecv.at[q], q)

    order = [*range(1, mids), 0]
    for q in order:
        pick(half + q * mid_rows, mid_rows)
        pair_sum(q).start()
    for q in order:
        pick(q * mid_rows, mid_rows)
        pair_sum(q).wait_recv()
        at = slice(q * mid_rows, (q + 1) * mid_rows)
        share[at, :] = share[at, :] + pair_in[at, :]
        if q:
            mid_sum(q).start()
    for q in range(1, mids):
        mid_sum(q).wait_recv()
    part = share[0:mid_rows, :]
    for q in range(1, mids):
        part = part + mid_in[q * mid_rows:(q + 1) * mid_rows, :]
    share[0:mid_rows, :] = part
    for q in range(1, fars):
        far_sum(q).start()
    for q in range(1, fars):
        far_sum(q).wait_recv()
    kept = share[0:far_rows, :]
    for q in range(1, fars):
        kept = kept + far_in[q * far_rows:(q + 1) * far_rows, :]
    gathered[0:far_rows, :] = kept * (1.0 / math.sqrt(rows * devices))

    def far_gather(q):
        return remote(gathered.at[pl.ds(0, far_rows), :], gathered.at[pl.ds(q * far_rows, far_rows), :],
                      gfsend.at[q], gfrecv.at[q], q)

    def mid_gather(q):
        return remote(gathered.at[pl.ds(0, mid_rows), :], gathered.at[pl.ds(q * mid_rows, mid_rows), :],
                      gmsend.at[q], gmrecv.at[q], q * fars)

    def pair_gather(q):
        return remote(gathered.at[pl.ds(q * mid_rows, mid_rows), :], gathered.at[pl.ds(half + q * mid_rows, mid_rows), :],
                      gpsend.at[q], gprecv.at[q], pair)

    for q in range(1, fars):
        far_gather(q).start()
    for q in range(1, fars):
        far_gather(q).wait_recv()
    for q in range(1, mids):
        mid_gather(q).start()
    pair_gather(0).start()
    for q in range(1, mids):
        mid_gather(q).wait_recv()
        pair_gather(q).start()

    def product(first, size):
        block = gathered[first:first + size, :]
        return lax.dot_general(block, block, (((0,), (0,)), ((), ())),
                               precision=HIGHEST, preferred_element_type=F32)

    def sketch():
        span = nl * count
        owners = notes[0:nl, :]
        k = lax.broadcasted_iota(jnp.int32, (nl, LANES), 1)
        mine = (owners == lo) & (k >= count) & (k < 2 * count)
        match = jnp.where(mine, 1.0, 0.0).astype(F32)
        up = lax.broadcasted_iota(jnp.int32, (LANES, LANES), 0)
        across = lax.broadcasted_iota(jnp.int32, (LANES, LANES), 1)
        ahead = jnp.where(up < across, 1.0, 0.0).astype(F32)
        before = jnp.dot(match, ahead, precision=HIGHEST, preferred_element_type=F32)
        spread_row = lax.broadcasted_iota(jnp.int32, (LANES, span), 0)
        spread_col = lax.broadcasted_iota(jnp.int32, (LANES, span), 1)
        spread = jnp.where(spread_row - count == spread_col % count, 1.0, 0.0).astype(F32)
        lead = lax.broadcasted_iota(jnp.int32, (nl, span), 0)
        cell = lax.broadcasted_iota(jnp.int32, (nl, span), 1)
        order_row = lax.broadcasted_iota(jnp.int32, (nl, nl), 0)
        order_col = lax.broadcasted_iota(jnp.int32, (nl, nl), 1)
        source = ((order_col << 1) & (nl - 1)) | (order_col >> (bl - 1))
        turn = jnp.where((source ^ lo) == order_row, 1.0, 0.0).astype(F32)
        rows_here = gathered[0:span, :]
        for m in range(MOST):
            chosen = jnp.where(jnp.abs(before - m) < 0.5, match, 0.0)
            wide = jnp.dot(chosen, spread, precision=HIGHEST, preferred_element_type=F32)
            wide = jnp.where(cell // count == lead, wide, 0.0)
            wide = jnp.dot(turn, wide, precision=HIGHEST, preferred_element_type=F32)
            sketch_ref[m, :, :] = jnp.dot(wide, rows_here, precision=HIGHEST,
                                          preferred_element_type=F32)

    sketch()
    gram = product(0, half)
    for q in range(mids):
        pair_gather(q).wait_recv()
    gram_ref[...] = (gram + product(half, half)) * (1.0 / total)

    for p in range(1, devices):
        note(p).wait_send()
    for q in range(mids):
        pair_sum(q).wait_send()
        pair_gather(q).wait_send()
    for q in range(1, mids):
        mid_sum(q).wait_send()
        mid_gather(q).wait_send()
    for q in range(1, fars):
        far_sum(q).wait_send()
        far_gather(q).wait_send()


def eliminate(both, hook):
    nb = both.shape[0]
    sub = lax.broadcasted_iota(jnp.int32, (8, both.shape[1]), 0)
    wide = (8, both.shape[1])
    tiles = [both[8 * g:8 * g + 8, :] for g in range(nb // 8)]
    for g0 in range(nb // 8):
        hook()
        cols = {}
        for g in range(g0, nb // 8):
            cols[g] = [jnp.broadcast_to(tiles[g][:, 8 * g0 + j:8 * g0 + j + 1], wide) for j in range(8)]
        for i in range(8):
            if i == 7 and g0 == nb // 8 - 1:
                break
            lead = cols[g0]
            flip = 1.0 / lead[i][i:i + 1, :]
            pivot = tiles[g0][i:i + 1, :]
            heads = [lead[j][i:i + 1, :] for j in range(8)]
            for g in range(g0, nb // 8):
                if g == g0 and i == 7:
                    continue
                rate = cols[g][i] * flip
                if g == g0:
                    rate = jnp.where(sub > i, rate, 0.0)
                for j in range(i + 1, 8):
                    cols[g][j] = cols[g][j] - rate * heads[j]
                tiles[g] = tiles[g] - rate * pivot
    return jnp.concatenate(tiles, axis=0)


def factor_kernel(gram_ref, sketch_in, current_ref, sketch_ref, r_ref, out_ref,
                  xbuf, parts, obuf, load_sem, store_sem):
    rows, width = current_ref.shape
    pieces = 8
    step = rows // pieces

    def load(c):
        at = pl.ds(c * step, step)
        return pltpu.make_async_copy(current_ref.at[at, :], xbuf.at[at, :], load_sem.at[c])

    def store(c):
        at = pl.ds(c * step, step)
        return pltpu.make_async_copy(obuf.at[at, :], out_ref.at[at, :], store_sem.at[c])

    for c in range(pieces):
        load(c).start()
    for source in range(sketch_ref.shape[0]):
        for m in range(MOST):
            sketch_ref[source, m:m + 1, :] = sketch_in[m, source:source + 1, :]

    n = width
    blocks = n // BLOCK
    hooks = blocks * (BLOCK // 8)
    slab = rows // (hooks - BLOCK // 8)
    state = {"next": 0, "turn": 0}

    def split():
        state["turn"] += 1
        if state["turn"] <= BLOCK // 8 or state["next"] >= rows:
            return
        first = state["next"]
        last = min(rows, first + -(-slab // 16) * 16)
        state["next"] = last
        x = xbuf[first:last, :]
        top = x.astype(BF16)
        parts[first:last, 0:width] = top
        parts[first:last, width:2 * width] = (x - top.astype(F32)).astype(BF16)

    row = lax.broadcasted_iota(jnp.int32, (BLOCK, n), 0)
    col = lax.broadcasted_iota(jnp.int32, (BLOCK, n), 1)
    a = [gram_ref[k * BLOCK:(k + 1) * BLOCK, :] for k in range(blocks)]
    w = [jnp.where(row + k * BLOCK == col, 1.0, 0.0).astype(F32) for k in range(blocks)]
    small_row = lax.broadcasted_iota(jnp.int32, (BLOCK, BLOCK), 0)
    small_col = lax.broadcasted_iota(jnp.int32, (BLOCK, BLOCK), 1)
    unit = jnp.where(small_row == small_col, 1.0, 0.0).astype(F32)
    for k in range(blocks):
        at = slice(k * BLOCK, (k + 1) * BLOCK)
        if k == 1:
            for c in range(pieces):
                load(c).wait()
        both = eliminate(jnp.concatenate([a[k][:, at], unit], axis=1), split)
        diag = jnp.sum(jnp.where(small_row == small_col, both[:, :BLOCK], 0.0), axis=1, keepdims=True)
        scale = 1.0 / jnp.sqrt(diag)
        inv = both[:, BLOCK:] * scale
        r_rows = jnp.dot(inv, a[k], precision=HIGHEST, preferred_element_type=F32)
        lower = {}
        for later in range(k + 1, blocks):
            lower[later] = lax.dot_general(a[later][:, at], inv, (((1,), (1,)), ((), ())),
                                           precision=HIGHEST, preferred_element_type=F32)
            a[later] = a[later] - jnp.dot(lower[later], r_rows, precision=HIGHEST,
                                          preferred_element_type=F32)
        w_rows = jnp.dot(inv, w[k], precision=HIGHEST, preferred_element_type=F32)
        for later in range(k + 1, blocks):
            w[later] = w[later] - jnp.dot(lower[later], w_rows, precision=HIGHEST,
                                          preferred_element_type=F32)
        r_ref[at, :] = jnp.where(row + k * BLOCK <= col, r_rows, 0.0)
        w[k] = w_rows
    inverse = jnp.concatenate(w, axis=0).T
    top = inverse.astype(BF16)
    rest = (inverse - top.astype(F32)).astype(BF16)
    stack = jnp.concatenate([top, top, rest], axis=0)
    for c in range(pieces):
        at = slice(c * step, (c + 1) * step)
        x = parts[at, :]
        x = jnp.concatenate([x, x[:, 0:width]], axis=1)
        obuf[at, :] = jnp.dot(x, stack, preferred_element_type=F32)
        store(c).start()
    for c in range(pieces):
        store(c).wait()


def shards(nh, nl, current, signs, sample_rows, sample_owner):
    rows, width = current.shape
    count = sample_rows.shape[0]
    devices = nh * nl
    total = devices * count
    vmem = pl.BlockSpec(memory_space=pltpu.VMEM)
    anywhere = pl.BlockSpec(memory_space=pl.ANY)
    dma = pltpu.SemaphoreType.DMA
    gram, picked = pl.pallas_call(
        functools.partial(mix_kernel, nh, nl, count),
        name="mix",
        out_shape=(jax.ShapeDtypeStruct((width, width), F32),
                   jax.ShapeDtypeStruct((MOST, nl, width), F32)),
        in_specs=[anywhere, anywhere, anywhere, anywhere],
        out_specs=(vmem, vmem),
        scratch_shapes=[
            pltpu.VMEM((1, count), jnp.int32),
            pltpu.VMEM((1, count), jnp.int32),
            pltpu.VMEM((rows // LANES, LANES), jnp.int32),
            pltpu.VMEM((1, LANES), jnp.int32),
            pltpu.VMEM((devices, LANES), jnp.int32),
            pltpu.SMEM((devices, LANES), jnp.int32),
            pltpu.VMEM((rows, width), F32),
            pltpu.VMEM((rows, width), F32),
            pltpu.VMEM((total, width), F32),
            pltpu.VMEM((total // 2, width), F32),
            pltpu.VMEM((total // 2, width), F32),
            pltpu.VMEM((nl // 2 * count, width), F32),
            pltpu.VMEM((total, width), F32),
            dma((3,)), dma((rows // TILE,)), dma, dma((devices,)), dma((devices,)),
            dma((nh,)), dma((nh,)), dma((nh,)), dma((nh,)), dma((nl // 2,)), dma((nl // 2,)),
            dma((nl // 2,)), dma((nl // 2,)), dma((nh,)), dma((nh,)), dma((nh,)), dma((nh,)),
        ],
        compiler_params=pltpu.CompilerParams(
            collective_id=0, has_side_effects=True, vmem_limit_bytes=VMEM_LIMIT),
    )(sample_rows.reshape(1, count), sample_owner.reshape(1, count), signs.reshape(rows // LANES, LANES), current)
    sketch, r_factor, precond = pl.pallas_call(
        factor_kernel,
        name="factor",
        out_shape=(jax.ShapeDtypeStruct((nl, MOST, width), F32),
                   jax.ShapeDtypeStruct((width, width), F32),
                   jax.ShapeDtypeStruct((rows, width), F32)),
        in_specs=[vmem, vmem, anywhere],
        out_specs=(vmem, vmem, anywhere),
        scratch_shapes=[
            pltpu.VMEM((rows, width), F32),
            pltpu.VMEM((rows, 2 * width), BF16),
            pltpu.VMEM((rows, width), F32),
            dma((8,)), dma((8,)),
        ],
        compiler_params=pltpu.CompilerParams(vmem_limit_bytes=VMEM_LIMIT),
    )(gram, picked, current)
    return (sketch.reshape(1, 1, nl, MOST, width), r_factor, precond)


def solution(mesh):
    placed = (P(("hi", "lo"), None), P(("hi", "lo")), P(("hi", "lo")), P(("hi", "lo"), None))
    return jax.shard_map(
        functools.partial(shards, mesh.shape["hi"], mesh.shape["lo"]),
        mesh=mesh,
        in_specs=placed,
        out_specs=(P("hi", "lo", None, None, None), P(), P(("hi", "lo"), None)),
        check_vma=False,
    )
```

```python
import functools
import math

import jax
import jax.numpy as jnp
from jax import lax
from jax.experimental import pallas as pl
from jax.experimental.pallas import tpu as pltpu
from jax.sharding import PartitionSpec as P

MOST = 2
LANES = 128
BLOCK = 64
TILE = 256
VMEM_LIMIT = 61 * 2 ** 20
MESH = pl.DeviceIdType.MESH
HIGHEST = lax.Precision.HIGHEST
F32 = jnp.float32
BF16 = jnp.bfloat16


def bits_of(size):
    return size.bit_length() - 1


def parity(value, top):
    shift = 1
    while shift * 2 < top:
        shift *= 2
    while shift >= 1:
        value = value ^ (value >> shift)
        shift //= 2
    return value & 1


def mix_kernel(nh, nl, count, rows_hbm, owner_hbm, signs_hbm, current_ref, gram_ref, sketch_ref,
               rows_ref, owner_ref, signs_ref, note_ref, notes, places, xbuf, ybuf, share, pair_in, chip_in, gathered,
               small_sem, load_sem, place_sem, nsend, nrecv, psend, precv, csend, crecv,
               gcsend, gcrecv, gpsend, gprecv):
    hi, lo = lax.axis_index("hi"), lax.axis_index("lo")
    bh, bl = bits_of(nh), bits_of(nl)
    devices = nh * nl
    rows, width = current_ref.shape
    total = devices * count
    loads = rows // TILE
    fars, mids = nl // 2, nh
    chips, group, half = fars * mids, mids * count, total // 2

    def masks(p):
        return (((p >> 1) & (nh // 2 - 1)) << 1 | (p >> (bl + bh - 1)),
                ((p >> bh) & (fars - 1)) << 1 | (p & 1))

    def peer(p):
        mask_hi, mask_lo = masks(p)
        return (hi ^ mask_hi, lo ^ mask_lo)

    def load(c):
        at = pl.ds(c * TILE, TILE)
        return pltpu.make_async_copy(current_ref.at[at, :], xbuf.at[at, :], load_sem.at[c])

    small = [pltpu.make_async_copy(source, target, small_sem.at[k])
             for k, (source, target) in enumerate(
                 ((rows_hbm, rows_ref), (owner_hbm, owner_ref), (signs_hbm, signs_ref)))]
    for copy in small:
        copy.start()
    barrier = pltpu.get_barrier_semaphore()
    for p in range(1, devices):
        pl.semaphore_signal(barrier, inc=1, device_id=peer(p), device_id_type=MESH)
    for c in range(loads):
        load(c).start()
    for copy in small:
        copy.wait()
    note_ref[...] = jnp.zeros_like(note_ref)
    note_ref[:, 0:count] = rows_ref[...]
    note_ref[:, count:2 * count] = owner_ref[...]

    up = lax.broadcasted_iota(jnp.int32, (TILE, TILE), 0)
    across = lax.broadcasted_iota(jnp.int32, (TILE, TILE), 1)
    table = (1 - 2 * parity(up & across, TILE)).astype(F32).astype(BF16)

    def transform(first, last):
        for c in range(first, last):
            load(c).wait()
        for c in range(first, last):
            at = slice(c * TILE, (c + 1) * TILE)
            lanes = TILE // LANES
            sign = jnp.concatenate([signs_ref[c * lanes + k:c * lanes + k + 1, :] for k in range(lanes)], axis=1)
            signed = table * sign.astype(F32).astype(BF16)
            x = xbuf[at, :]
            top = x.astype(BF16)
            rest = (x - top.astype(F32)).astype(BF16)
            ybuf[at, :] = jnp.dot(jnp.concatenate([signed, signed], axis=1), jnp.concatenate([top, rest], axis=0),
                                  preferred_element_type=F32)

    transform(0, loads // 2)
    transform(loads // 2, loads)
    pl.semaphore_wait(barrier, devices - 1)

    def note(p):
        return pltpu.make_async_remote_copy(
            src_ref=note_ref, dst_ref=notes.at[pl.ds(p, 1), :],
            send_sem=nsend.at[p], recv_sem=nrecv.at[p],
            device_id=peer(p), device_id_type=MESH)

    for p in reversed(range(1, devices)):
        note(p).start()
    notes[0:1, :] = note_ref[...]

    @pl.loop(0, TILE // 8)
    def _(r):
        first = pl.multiple_of(r * 8, 8)
        block = [ybuf[pl.ds(first + c * TILE, 8), :] for c in range(loads)]
        step = 1
        while step < loads:
            block = [block[c] + block[c + step] if not c & step else block[c - step] - block[c]
                     for c in range(loads)]
            step *= 2
        for c in range(loads):
            xbuf[pl.ds(first + c * TILE, 8), :] = block[c]

    for p in range(1, devices):
        note(p).wait_recv()
    spread = pltpu.make_async_copy(notes, places, place_sem)
    spread.start()
    spread.wait()

    def pick(first, size):
        @pl.loop(first // count, (first + size) // count)
        def _(p):
            mask_hi, mask_lo = masks(p)
            odd = parity(((hi & ~mask_hi) << bl) | (lo & ~mask_lo), devices)
            flip = (1 - 2 * odd).astype(F32)
            base = pl.multiple_of(p * count, count)
            for i in range(count):
                share[pl.ds(base + i, 1), :] = xbuf[pl.ds(places[p, i], 1), :] * flip

    def sketch_tables():
        span = nl * count
        owners = jnp.concatenate([notes[q * mids:q * mids + 2, :] for q in range(fars)], axis=0)
        k = lax.broadcasted_iota(jnp.int32, (nl, LANES), 1)
        mine = (owners == lo) & (k >= count) & (k < 2 * count)
        match = jnp.where(mine, 1.0, 0.0).astype(F32)
        up = lax.broadcasted_iota(jnp.int32, (LANES, LANES), 0)
        across = lax.broadcasted_iota(jnp.int32, (LANES, LANES), 1)
        ahead = jnp.where(up < across, 1.0, 0.0).astype(F32)
        before = jnp.dot(match, ahead, precision=HIGHEST, preferred_element_type=F32)
        spread_row = lax.broadcasted_iota(jnp.int32, (LANES, span), 0)
        spread_col = lax.broadcasted_iota(jnp.int32, (LANES, span), 1)
        spread = jnp.where(spread_row - count == spread_col % count, 1.0, 0.0).astype(F32)
        lead = lax.broadcasted_iota(jnp.int32, (nl, span), 0)
        cell = lax.broadcasted_iota(jnp.int32, (nl, span), 1)
        order_row = lax.broadcasted_iota(jnp.int32, (nl, nl), 0)
        order_col = lax.broadcasted_iota(jnp.int32, (nl, nl), 1)
        turn = jnp.where((order_col ^ lo) == order_row, 1.0, 0.0).astype(F32)
        made = []
        for m in range(MOST):
            chosen = jnp.where(jnp.abs(before - m) < 0.5, match, 0.0)
            wide = jnp.dot(chosen, spread, precision=HIGHEST, preferred_element_type=F32)
            wide = jnp.where(cell // count == lead, wide, 0.0)
            made.append(jnp.dot(turn, wide, precision=HIGHEST, preferred_element_type=F32))
        return made

    def remote(source, target, send, recv, p):
        return pltpu.make_async_remote_copy(src_ref=source, dst_ref=target, send_sem=send, recv_sem=recv,
                                            device_id=peer(p), device_id_type=MESH)

    pair = devices // 2

    def block(ref, p):
        return ref.at[pl.ds(p * count, count), :]

    def groups(ref, q):
        return ref.at[pl.ds(q * group, group), :]

    def pair_sum(q):
        return remote(groups(share, fars + q), groups(pair_in, q), psend.at[q], precv.at[q], pair)

    def chip_sum(p):
        return remote(block(share, p), block(chip_in, p), csend.at[p], crecv.at[p], p)

    def chip_gather(p):
        return remote(block(gathered, 0), block(gathered, p), gcsend.at[p], gcrecv.at[p], p)

    def pair_gather(q):
        return remote(groups(gathered, q), groups(gathered, fars + q), gpsend.at[q], gprecv.at[q], pair)

    for q in reversed(range(fars)):
        pick(half + q * group, group)
        pair_sum(q).start()
    for q in reversed(range(fars)):
        pick(q * group, group)
        pair_sum(q).wait_recv()
        at = slice(q * group, (q + 1) * group)
        share[at, :] = share[at, :] + pair_in[at, :]
        for p in reversed(range(max(q * mids, 1), (q + 1) * mids)):
            chip_sum(p).start()
    tables = sketch_tables()
    kept = share[0:count, :]
    for p in range(1, chips):
        chip_sum(p).wait_recv()
        kept = kept + chip_in[p * count:(p + 1) * count, :]
    gathered[0:count, :] = kept * (1.0 / math.sqrt(rows * devices))
    for p in reversed(range(1, chips)):
        chip_gather(p).start()
    for q in range(fars):
        for p in range(max(q * mids, 1), (q + 1) * mids):
            chip_gather(p).wait_recv()
        pair_gather(q).start()

    def product(first, size):
        block = gathered[first:first + size, :]
        return lax.dot_general(block, block, (((0,), (0,)), ((), ())),
                               precision=HIGHEST, preferred_element_type=F32)

    gram = product(0, half)
    rows_here = jnp.concatenate([gathered[q * group:q * group + 2 * count, :] for q in range(fars)], axis=0)
    for m in range(MOST):
        sketch_ref[m, :, :] = jnp.dot(tables[m], rows_here, precision=HIGHEST, preferred_element_type=F32)
    for q in range(fars):
        pair_gather(q).wait_recv()
    gram_ref[...] = (gram + product(half, half)) * (1.0 / total)

    for p in range(1, devices):
        note(p).wait_send()
    for q in range(fars):
        pair_sum(q).wait_send()
        pair_gather(q).wait_send()
    for p in range(1, chips):
        chip_sum(p).wait_send()
        chip_gather(p).wait_send()


def eliminate(both, hook):
    nb = both.shape[0]
    sub = lax.broadcasted_iota(jnp.int32, (8, both.shape[1]), 0)
    wide = (8, both.shape[1])
    tiles = [both[8 * g:8 * g + 8, :] for g in range(nb // 8)]
    for g0 in range(nb // 8):
        hook()
        cols = {}
        for g in range(g0, nb // 8):
            cols[g] = [jnp.broadcast_to(tiles[g][:, 8 * g0 + j:8 * g0 + j + 1], wide) for j in range(8)]
        for i in range(8):
            if i == 7 and g0 == nb // 8 - 1:
                break
            lead = cols[g0]
            flip = 1.0 / lead[i][i:i + 1, :]
            pivot = tiles[g0][i:i + 1, :]
            heads = [lead[j][i:i + 1, :] for j in range(8)]
            for g in range(g0, nb // 8):
                if g == g0 and i == 7:
                    continue
                rate = cols[g][i] * flip
                if g == g0:
                    rate = jnp.where(sub > i, rate, 0.0)
                for j in range(i + 1, 8):
                    cols[g][j] = cols[g][j] - rate * heads[j]
                tiles[g] = tiles[g] - rate * pivot
    return jnp.concatenate(tiles, axis=0)


def factor_kernel(gram_ref, sketch_in, current_ref, sketch_ref, r_ref, out_ref,
                  xbuf, parts, obuf, load_sem, store_sem):
    rows, width = current_ref.shape
    pieces = 8
    step = rows // pieces

    def load(c):
        at = pl.ds(c * step, step)
        return pltpu.make_async_copy(current_ref.at[at, :], xbuf.at[at, :], load_sem.at[c])

    def store(c):
        at = pl.ds(c * step, step)
        return pltpu.make_async_copy(obuf.at[at, :], out_ref.at[at, :], store_sem.at[c])

    for c in range(pieces):
        load(c).start()
    for source in range(sketch_ref.shape[0]):
        for m in range(MOST):
            sketch_ref[source, m:m + 1, :] = sketch_in[m, source:source + 1, :]

    n = width
    blocks = n // BLOCK
    hooks = blocks * (BLOCK // 8)
    slab = rows // (hooks - BLOCK // 8)
    state = {"next": 0, "turn": 0}

    def split():
        state["turn"] += 1
        if state["turn"] <= BLOCK // 8 or state["next"] >= rows:
            return
        first = state["next"]
        last = min(rows, first + -(-slab // 16) * 16)
        state["next"] = last
        x = xbuf[first:last, :]
        top = x.astype(BF16)
        parts[first:last, 0:width] = top
        parts[first:last, width:2 * width] = (x - top.astype(F32)).astype(BF16)

    row = lax.broadcasted_iota(jnp.int32, (BLOCK, n), 0)
    col = lax.broadcasted_iota(jnp.int32, (BLOCK, n), 1)
    a = [gram_ref[k * BLOCK:(k + 1) * BLOCK, :] for k in range(blocks)]
    w = [jnp.where(row + k * BLOCK == col, 1.0, 0.0).astype(F32) for k in range(blocks)]
    small_row = lax.broadcasted_iota(jnp.int32, (BLOCK, BLOCK), 0)
    small_col = lax.broadcasted_iota(jnp.int32, (BLOCK, BLOCK), 1)
    unit = jnp.where(small_row == small_col, 1.0, 0.0).astype(F32)
    for k in range(blocks):
        at = slice(k * BLOCK, (k + 1) * BLOCK)
        if k == 1:
            for c in range(pieces):
                load(c).wait()
        both = eliminate(jnp.concatenate([a[k][:, at], unit], axis=1), split)
        diag = jnp.sum(jnp.where(small_row == small_col, both[:, :BLOCK], 0.0), axis=1, keepdims=True)
        scale = 1.0 / jnp.sqrt(diag)
        inv = both[:, BLOCK:] * scale
        r_rows = jnp.dot(inv, a[k], precision=HIGHEST, preferred_element_type=F32)
        lower = {}
        for later in range(k + 1, blocks):
            lower[later] = lax.dot_general(a[later][:, at], inv, (((1,), (1,)), ((), ())),
                                           precision=HIGHEST, preferred_element_type=F32)
            a[later] = a[later] - jnp.dot(lower[later], r_rows, precision=HIGHEST,
                                          preferred_element_type=F32)
        w_rows = jnp.dot(inv, w[k], precision=HIGHEST, preferred_element_type=F32)
        for later in range(k + 1, blocks):
            w[later] = w[later] - jnp.dot(lower[later], w_rows, precision=HIGHEST,
                                          preferred_element_type=F32)
        r_ref[at, :] = jnp.where(row + k * BLOCK <= col, r_rows, 0.0)
        w[k] = w_rows
    inverse = jnp.concatenate(w, axis=0).T
    top = inverse.astype(BF16)
    rest = (inverse - top.astype(F32)).astype(BF16)
    stack = jnp.concatenate([top, top, rest], axis=0)
    for c in range(pieces):
        at = slice(c * step, (c + 1) * step)
        x = parts[at, :]
        x = jnp.concatenate([x, x[:, 0:width]], axis=1)
        obuf[at, :] = jnp.dot(x, stack, preferred_element_type=F32)
        store(c).start()
    for c in range(pieces):
        store(c).wait()


def shards(nh, nl, current, signs, sample_rows, sample_owner):
    rows, width = current.shape
    count = sample_rows.shape[0]
    devices = nh * nl
    total = devices * count
    vmem = pl.BlockSpec(memory_space=pltpu.VMEM)
    anywhere = pl.BlockSpec(memory_space=pl.ANY)
    dma = pltpu.SemaphoreType.DMA
    gram, picked = pl.pallas_call(
        functools.partial(mix_kernel, nh, nl, count),
        name="mix",
        out_shape=(jax.ShapeDtypeStruct((width, width), F32),
                   jax.ShapeDtypeStruct((MOST, nl, width), F32)),
        in_specs=[anywhere, anywhere, anywhere, anywhere],
        out_specs=(vmem, vmem),
        scratch_shapes=[
            pltpu.VMEM((1, count), jnp.int32),
            pltpu.VMEM((1, count), jnp.int32),
            pltpu.VMEM((rows // LANES, LANES), jnp.int32),
            pltpu.VMEM((1, LANES), jnp.int32),
            pltpu.VMEM((devices, LANES), jnp.int32),
            pltpu.SMEM((devices, LANES), jnp.int32),
            pltpu.VMEM((rows, width), F32),
            pltpu.VMEM((rows, width), F32),
            pltpu.VMEM((total, width), F32),
            pltpu.VMEM((total // 2, width), F32),
            pltpu.VMEM((total // 2, width), F32),
            pltpu.VMEM((total, width), F32),
            dma((3,)), dma((rows // TILE,)), dma, dma((devices,)), dma((devices,)),
            dma((nl // 2,)), dma((nl // 2,)), dma((devices // 2,)), dma((devices // 2,)),
            dma((devices // 2,)), dma((devices // 2,)), dma((nl // 2,)), dma((nl // 2,)),
        ],
        compiler_params=pltpu.CompilerParams(
            collective_id=0, has_side_effects=True, vmem_limit_bytes=VMEM_LIMIT),
    )(sample_rows.reshape(1, count), sample_owner.reshape(1, count), signs.reshape(rows // LANES, LANES), current)
    sketch, r_factor, precond = pl.pallas_call(
        factor_kernel,
        name="factor",
        out_shape=(jax.ShapeDtypeStruct((nl, MOST, width), F32),
                   jax.ShapeDtypeStruct((width, width), F32),
                   jax.ShapeDtypeStruct((rows, width), F32)),
        in_specs=[vmem, vmem, anywhere],
        out_specs=(vmem, vmem, anywhere),
        scratch_shapes=[
            pltpu.VMEM((rows, width), F32),
            pltpu.VMEM((rows, 2 * width), BF16),
            pltpu.VMEM((rows, width), F32),
            dma((8,)), dma((8,)),
        ],
        compiler_params=pltpu.CompilerParams(vmem_limit_bytes=VMEM_LIMIT),
    )(gram, picked, current)
    return (sketch.reshape(1, 1, nl, MOST, width), r_factor, precond)


def solution(mesh):
    placed = (P(("hi", "lo"), None), P(("hi", "lo")), P(("hi", "lo")), P(("hi", "lo"), None))
    return jax.shard_map(
        functools.partial(shards, mesh.shape["hi"], mesh.shape["lo"]),
        mesh=mesh,
        in_specs=placed,
        out_specs=(P("hi", "lo", None, None, None), P(), P(("hi", "lo"), None)),
        check_vma=False,
    )
```

```python
import functools
import math

import jax
import jax.numpy as jnp
from jax import lax
from jax.experimental import pallas as pl
from jax.experimental.pallas import tpu as pltpu
from jax.sharding import PartitionSpec as P

MOST = 2
LANES = 128
BLOCK = 64
TILE = 256
VMEM_LIMIT = 61 * 2 ** 20
MESH = pl.DeviceIdType.MESH
HIGHEST = lax.Precision.HIGHEST
F32 = jnp.float32
BF16 = jnp.bfloat16


def bits_of(size):
    return size.bit_length() - 1


def parity(value, top):
    shift = 1
    while shift * 2 < top:
        shift *= 2
    while shift >= 1:
        value = value ^ (value >> shift)
        shift //= 2
    return value & 1


def mix_kernel(nh, nl, count, rows_hbm, owner_hbm, signs_hbm, current_ref, gram_ref, sketch_ref,
               rows_ref, owner_ref, signs_ref, note_ref, notes, places, xbuf, ybuf, share, pair_in, chip_in, gathered,
               small_sem, load_sem, place_sem, nsend, nrecv, psend, precv, csend, crecv,
               gcsend, gcrecv, gpsend, gprecv):
    hi, lo = lax.axis_index("hi"), lax.axis_index("lo")
    bh, bl = bits_of(nh), bits_of(nl)
    devices = nh * nl
    rows, width = current_ref.shape
    total = devices * count
    loads = rows // TILE
    fars, mids = nl // 2, nh
    chips, group, half = fars * mids, mids * count, total // 2

    def masks(p):
        return (((p >> 1) & (nh // 2 - 1)) << 1 | (p >> (bl + bh - 1)),
                ((p >> bh) & (fars - 1)) << 1 | (p & 1))

    def peer(p):
        mask_hi, mask_lo = masks(p)
        return (hi ^ mask_hi, lo ^ mask_lo)

    def load(c):
        at = pl.ds(c * TILE, TILE)
        return pltpu.make_async_copy(current_ref.at[at, :], xbuf.at[at, :], load_sem.at[c])

    small = [pltpu.make_async_copy(source, target, small_sem.at[k])
             for k, (source, target) in enumerate(
                 ((rows_hbm, rows_ref), (owner_hbm, owner_ref), (signs_hbm, signs_ref)))]
    for copy in small:
        copy.start()
    barrier = pltpu.get_barrier_semaphore()
    for p in range(1, devices):
        pl.semaphore_signal(barrier, inc=1, device_id=peer(p), device_id_type=MESH)
    for c in range(loads):
        load(c).start()
    for copy in small:
        copy.wait()
    note_ref[...] = jnp.zeros_like(note_ref)
    note_ref[:, 0:count] = rows_ref[...]
    note_ref[:, count:2 * count] = owner_ref[...]

    up = lax.broadcasted_iota(jnp.int32, (TILE, TILE), 0)
    across = lax.broadcasted_iota(jnp.int32, (TILE, TILE), 1)
    table = (1 - 2 * parity(up & across, TILE)).astype(F32).astype(BF16)

    def transform(first, last):
        for c in range(first, last):
            load(c).wait()
        for c in range(first, last):
            at = slice(c * TILE, (c + 1) * TILE)
            lanes = TILE // LANES
            sign = jnp.concatenate([signs_ref[c * lanes + k:c * lanes + k + 1, :] for k in range(lanes)], axis=1)
            signed = table * sign.astype(F32).astype(BF16)
            x = xbuf[at, :]
            top = x.astype(BF16)
            rest = (x - top.astype(F32)).astype(BF16)
            ybuf[at, :] = jnp.dot(jnp.concatenate([signed, signed], axis=1), jnp.concatenate([top, rest], axis=0),
                                  preferred_element_type=F32)

    transform(0, loads // 2)
    transform(loads // 2, loads)
    pl.semaphore_wait(barrier, devices - 1)

    def note(p):
        return pltpu.make_async_remote_copy(
            src_ref=note_ref, dst_ref=notes.at[pl.ds(p, 1), :],
            send_sem=nsend.at[p], recv_sem=nrecv.at[p],
            device_id=peer(p), device_id_type=MESH)

    for p in reversed(range(1, devices)):
        note(p).start()
    notes[0:1, :] = note_ref[...]

    @pl.loop(0, TILE // 8)
    def _(r):
        first = pl.multiple_of(r * 8, 8)
        block = [ybuf[pl.ds(first + c * TILE, 8), :] for c in range(loads)]
        step = 1
        while step < loads:
            block = [block[c] + block[c + step] if not c & step else block[c - step] - block[c]
                     for c in range(loads)]
            step *= 2
        for c in range(loads):
            xbuf[pl.ds(first + c * TILE, 8), :] = block[c]

    for p in range(1, devices):
        note(p).wait_recv()
    spread = pltpu.make_async_copy(notes, places, place_sem)
    spread.start()
    spread.wait()

    def pick(first, size):
        @pl.loop(first // count, (first + size) // count)
        def _(p):
            mask_hi, mask_lo = masks(p)
            odd = parity(((hi & ~mask_hi) << bl) | (lo & ~mask_lo), devices)
            flip = (1 - 2 * odd).astype(F32)
            base = pl.multiple_of(p * count, count)
            for i in range(count):
                share[pl.ds(base + i, 1), :] = xbuf[pl.ds(places[p, i], 1), :] * flip

    def sketch_tables():
        span = nl * count
        owners = jnp.concatenate([notes[q * mids:q * mids + 2, :] for q in range(fars)], axis=0)
        k = lax.broadcasted_iota(jnp.int32, (nl, LANES), 1)
        mine = (owners == lo) & (k >= count) & (k < 2 * count)
        match = jnp.where(mine, 1.0, 0.0).astype(F32)
        up = lax.broadcasted_iota(jnp.int32, (LANES, LANES), 0)
        across = lax.broadcasted_iota(jnp.int32, (LANES, LANES), 1)
        ahead = jnp.where(up < across, 1.0, 0.0).astype(F32)
        before = jnp.dot(match, ahead, precision=HIGHEST, preferred_element_type=F32)
        spread_row = lax.broadcasted_iota(jnp.int32, (LANES, span), 0)
        spread_col = lax.broadcasted_iota(jnp.int32, (LANES, span), 1)
        spread = jnp.where(spread_row - count == spread_col % count, 1.0, 0.0).astype(F32)
        lead = lax.broadcasted_iota(jnp.int32, (nl, span), 0)
        cell = lax.broadcasted_iota(jnp.int32, (nl, span), 1)
        order_row = lax.broadcasted_iota(jnp.int32, (nl, nl), 0)
        order_col = lax.broadcasted_iota(jnp.int32, (nl, nl), 1)
        turn = jnp.where((order_col ^ lo) == order_row, 1.0, 0.0).astype(F32)
        made = []
        for m in range(MOST):
            chosen = jnp.where(jnp.abs(before - m) < 0.5, match, 0.0)
            wide = jnp.dot(chosen, spread, precision=HIGHEST, preferred_element_type=F32)
            wide = jnp.where(cell // count == lead, wide, 0.0)
            made.append(jnp.dot(turn, wide, precision=HIGHEST, preferred_element_type=F32))
        return made

    def remote(source, target, send, recv, p):
        return pltpu.make_async_remote_copy(src_ref=source, dst_ref=target, send_sem=send, recv_sem=recv,
                                            device_id=peer(p), device_id_type=MESH)

    pair = devices // 2

    def block(ref, p):
        return ref.at[pl.ds(p * count, count), :]

    def groups(ref, q):
        return ref.at[pl.ds(q * group, group), :]

    def pair_sum(q):
        return remote(groups(share, fars + q), groups(pair_in, q), psend.at[q], precv.at[q], pair)

    def chip_sum(p):
        return remote(block(share, p), block(chip_in, p), csend.at[p], crecv.at[p], p)

    def chip_gather(p):
        return remote(block(gathered, 0), block(gathered, p), gcsend.at[p], gcrecv.at[p], p)

    def pair_gather(q):
        return remote(groups(gathered, q), groups(gathered, fars + q), gpsend.at[q], gprecv.at[q], pair)

    for q in reversed(range(fars)):
        pick(half + q * group, group)
        pair_sum(q).start()
    for q in reversed(range(fars)):
        pick(q * group, group)
        pair_sum(q).wait_recv()
        at = slice(q * group, (q + 1) * group)
        share[at, :] = share[at, :] + pair_in[at, :]
        for p in reversed(range(max(q * mids, 1), (q + 1) * mids)):
            chip_sum(p).start()
    tables = sketch_tables()
    kept = share[0:count, :]
    for p in range(1, chips):
        chip_sum(p).wait_recv()
        kept = kept + chip_in[p * count:(p + 1) * count, :]
    gathered[0:count, :] = kept * (1.0 / math.sqrt(rows * devices))
    for p in reversed(range(1, chips)):
        chip_gather(p).start()
    for q in range(fars):
        for p in range(max(q * mids, 1), (q + 1) * mids):
            chip_gather(p).wait_recv()
        pair_gather(q).start()

    def product(first, size):
        block = gathered[first:first + size, :]
        return lax.dot_general(block, block, (((0,), (0,)), ((), ())),
                               precision=HIGHEST, preferred_element_type=F32)

    gram = product(0, half)
    rows_here = jnp.concatenate([gathered[q * group:q * group + 2 * count, :] for q in range(fars)], axis=0)
    for m in range(MOST):
        sketch_ref[m, :, :] = jnp.dot(tables[m], rows_here, precision=HIGHEST, preferred_element_type=F32)
    for q in range(fars):
        pair_gather(q).wait_recv()
    gram_ref[...] = (gram + product(half, half)) * (1.0 / total)

    for p in range(1, devices):
        note(p).wait_send()
    for q in range(fars):
        pair_sum(q).wait_send()
        pair_gather(q).wait_send()
    for p in range(1, chips):
        chip_sum(p).wait_send()
        chip_gather(p).wait_send()


def eliminate(both, hook):
    nb = both.shape[0]
    sub = lax.broadcasted_iota(jnp.int32, (8, both.shape[1]), 0)
    wide = (8, both.shape[1])
    tiles = [both[8 * g:8 * g + 8, :] for g in range(nb // 8)]
    for g0 in range(nb // 8):
        hook()
        cols = {}
        for g in range(g0, nb // 8):
            cols[g] = [jnp.broadcast_to(tiles[g][:, 8 * g0 + j:8 * g0 + j + 1], wide) for j in range(8)]
        for i in range(8):
            if i == 7 and g0 == nb // 8 - 1:
                break
            lead = cols[g0]
            flip = 1.0 / lead[i][i:i + 1, :]
            pivot = tiles[g0][i:i + 1, :]
            heads = [lead[j][i:i + 1, :] for j in range(8)]
            for g in range(g0, nb // 8):
                if g == g0 and i == 7:
                    continue
                rate = cols[g][i] * flip
                if g == g0:
                    rate = jnp.where(sub > i, rate, 0.0)
                for j in range(i + 1, 8):
                    cols[g][j] = cols[g][j] - rate * heads[j]
                tiles[g] = tiles[g] - rate * pivot
    return jnp.concatenate(tiles, axis=0)


def three(value):
    top = value.astype(BF16)
    value = value - top.astype(F32)
    mid = value.astype(BF16)
    return top, mid, (value - mid.astype(F32)).astype(BF16)


def factor_kernel(gram_ref, sketch_in, current_ref, sketch_ref, r_ref, out_ref,
                  xbuf, parts, obuf, load_sem, store_sem):
    rows, width = current_ref.shape
    blocks = width // BLOCK
    turns = width // 32
    pieces = turns
    step = rows // pieces
    wide = width // 2

    def load(c):
        at = pl.ds(c * step, step)
        return pltpu.make_async_copy(current_ref.at[at, :], xbuf.at[at, :], load_sem.at[c])

    def store(c, side):
        at = (pl.ds(c * step, step), pl.ds(side * wide, wide))
        return pltpu.make_async_copy(obuf.at[at], out_ref.at[at], store_sem.at[c, side])

    for c in range(pieces):
        load(c).start()
    for source in range(sketch_ref.shape[0]):
        for m in range(MOST):
            sketch_ref[source, m:m + 1, :] = sketch_in[m, source:source + 1, :]

    def split(c):
        load(c).wait()
        at = slice(c * step, (c + 1) * step)
        x = xbuf[at, :]
        top = x.astype(BF16)
        rest = (x - top.astype(F32)).astype(BF16)
        parts[at, 0:wide] = top[:, 0:wide]
        parts[at, wide:2 * wide] = rest[:, 0:wide]
        parts[at, 2 * wide:3 * wide] = top[:, wide:]
        parts[at, 3 * wide:] = rest[:, wide:]

    def turned(inverse):
        inverse = inverse.T
        top = inverse.astype(BF16)
        rest = (inverse - top.astype(F32)).astype(BF16)
        both = jnp.concatenate([top, rest], axis=1)
        return jnp.concatenate([both[k * wide:(k + 1) * wide, :]
                                for k in range(both.shape[0] // wide) for _ in range(2)], axis=0)

    def solve(first, last, stack, side):
        x = parts[first:last, 0:stack.shape[0]]
        both = jnp.dot(x, stack, preferred_element_type=F32)
        obuf[first:last, side * wide:(side + 1) * wide] = both[:, 0:wide] + both[:, wide:]

    state = {"turn": 0, "stack": None}

    def hook():
        turn = state["turn"]
        state["turn"] += 1
        if turns <= turn < 2 * turns:
            split(turn - turns)
        elif turn >= 2 * turns:
            turn -= 2 * turns
            half = step // 2
            solve(turn * half, (turn + 1) * half, state["stack"], 0)
            if turn % 2:
                store(turn // 2, 0).start()

    size = (BLOCK, LANES)
    row = lax.broadcasted_iota(jnp.int32, size, 0)
    lane = lax.broadcasted_iota(jnp.int32, size, 1)
    halves = range(width // LANES)
    left_half = lane < BLOCK
    unit = jnp.where(row == lane - BLOCK, 1.0, 0.0).astype(F32)
    a = [[gram_ref[k * BLOCK:(k + 1) * BLOCK, h * LANES:(h + 1) * LANES] for h in halves] for k in range(blocks)]
    inverse = []
    for k in range(blocks):
        first, last = k * BLOCK, (k + 1) * BLOCK
        if k == blocks // 2:
            state["stack"] = turned(jnp.concatenate(inverse, axis=0)[:, 0:wide])
        home, start = first // LANES, first % LANES
        own = a[k][home]
        if start:
            own = pltpu.roll(own, BLOCK, 1)
        both = eliminate(jnp.where(left_half, own, unit), hook)
        diag = jnp.sum(jnp.where(row == lane, both, 0.0), axis=1, keepdims=True)
        both = both * (1.0 / jnp.sqrt(diag))
        both = jnp.where(left_half, pltpu.roll(both, BLOCK, 1), both)
        top, mid, low = [part.astype(F32) for part in three(both)]
        left = jnp.concatenate([top, jnp.where(left_half, top, mid), jnp.where(left_half, mid, low)], axis=1).astype(BF16)
        top, mid, low = three(jnp.concatenate(a[k], axis=1))
        right = jnp.concatenate([top, mid, low, top, mid, top], axis=0)
        done = jnp.dot(left, right, preferred_element_type=F32)
        done = [done[:, h * LANES:(h + 1) * LANES] for h in halves]
        for h in halves:
            r_ref[first:last, h * LANES:(h + 1) * LANES] = jnp.where(row + first <= lane + h * LANES, done[h], 0.0)
        inside = (lane >= start) & (lane < start + BLOCK)
        done[home] = jnp.where(inside, both, done[home])
        inverse.append(jnp.concatenate([jnp.where(lane + h * LANES < last, done[h], 0.0) for h in halves], axis=1))
        if k == blocks - 1:
            break
        top, mid, low = three(jnp.concatenate(done, axis=1))
        base = last // LANES * LANES
        left = jnp.concatenate([top, top, mid, top, low, mid], axis=0)[:, base:]
        right = jnp.concatenate([top, mid, top, low, top, mid], axis=0)
        change = lax.dot_general(left, right, (((0,), (0,)), ((), ())), preferred_element_type=F32)
        for later in range(k + 1, blocks):
            at = later * BLOCK - base
            for h in halves:
                old = jnp.where(inside, 0.0, a[later][h]) if h == home else a[later][h]
                a[later][h] = old - change[at:at + BLOCK, h * LANES:(h + 1) * LANES]
    stack = turned(jnp.concatenate(inverse[blocks // 2:], axis=0))
    for c in range(pieces):
        solve(c * step, (c + 1) * step, stack, 1)
        store(c, 1).start()
    for c in range(pieces):
        store(c, 0).wait()
        store(c, 1).wait()


def shards(nh, nl, current, signs, sample_rows, sample_owner):
    rows, width = current.shape
    count = sample_rows.shape[0]
    devices = nh * nl
    total = devices * count
    vmem = pl.BlockSpec(memory_space=pltpu.VMEM)
    anywhere = pl.BlockSpec(memory_space=pl.ANY)
    dma = pltpu.SemaphoreType.DMA
    gram, picked = pl.pallas_call(
        functools.partial(mix_kernel, nh, nl, count),
        name="mix",
        out_shape=(jax.ShapeDtypeStruct((width, width), F32),
                   jax.ShapeDtypeStruct((MOST, nl, width), F32)),
        in_specs=[anywhere, anywhere, anywhere, anywhere],
        out_specs=(vmem, vmem),
        scratch_shapes=[
            pltpu.VMEM((1, count), jnp.int32),
            pltpu.VMEM((1, count), jnp.int32),
            pltpu.VMEM((rows // LANES, LANES), jnp.int32),
            pltpu.VMEM((1, LANES), jnp.int32),
            pltpu.VMEM((devices, LANES), jnp.int32),
            pltpu.SMEM((devices, LANES), jnp.int32),
            pltpu.VMEM((rows, width), F32),
            pltpu.VMEM((rows, width), F32),
            pltpu.VMEM((total, width), F32),
            pltpu.VMEM((total // 2, width), F32),
            pltpu.VMEM((total // 2, width), F32),
            pltpu.VMEM((total, width), F32),
            dma((3,)), dma((rows // TILE,)), dma, dma((devices,)), dma((devices,)),
            dma((nl // 2,)), dma((nl // 2,)), dma((devices // 2,)), dma((devices // 2,)),
            dma((devices // 2,)), dma((devices // 2,)), dma((nl // 2,)), dma((nl // 2,)),
        ],
        compiler_params=pltpu.CompilerParams(
            collective_id=0, has_side_effects=True, vmem_limit_bytes=VMEM_LIMIT),
    )(sample_rows.reshape(1, count), sample_owner.reshape(1, count), signs.reshape(rows // LANES, LANES), current)
    sketch, r_factor, precond = pl.pallas_call(
        factor_kernel,
        name="factor",
        out_shape=(jax.ShapeDtypeStruct((nl, MOST, width), F32),
                   jax.ShapeDtypeStruct((width, width), F32),
                   jax.ShapeDtypeStruct((rows, width), F32)),
        in_specs=[vmem, vmem, anywhere],
        out_specs=(vmem, vmem, anywhere),
        scratch_shapes=[
            pltpu.VMEM((rows, width), F32),
            pltpu.VMEM((rows, 2 * width), BF16),
            pltpu.VMEM((rows, width), F32),
            dma((width // 32,)), dma((width // 32, 2)),
        ],
        compiler_params=pltpu.CompilerParams(vmem_limit_bytes=VMEM_LIMIT),
    )(gram, picked, current)
    return (sketch.reshape(1, 1, nl, MOST, width), r_factor, precond)


def solution(mesh):
    placed = (P(("hi", "lo"), None), P(("hi", "lo")), P(("hi", "lo")), P(("hi", "lo"), None))
    return jax.shard_map(
        functools.partial(shards, mesh.shape["hi"], mesh.shape["lo"]),
        mesh=mesh,
        in_specs=placed,
        out_specs=(P("hi", "lo", None, None, None), P(), P(("hi", "lo"), None)),
        check_vma=False,
    )
```

```python
import functools
import math

import jax
import jax.numpy as jnp
from jax import lax
from jax.experimental import pallas as pl
from jax.experimental.pallas import tpu as pltpu
from jax.sharding import PartitionSpec as P

MOST = 2
LANES = 128
BLOCK = 64
TILE = 256
VMEM_LIMIT = 61 * 2 ** 20
MESH = pl.DeviceIdType.MESH
HIGHEST = lax.Precision.HIGHEST
F32 = jnp.float32
BF16 = jnp.bfloat16


def bits_of(size):
    return size.bit_length() - 1


def parity(value, top):
    shift = 1
    while shift * 2 < top:
        shift *= 2
    while shift >= 1:
        value = value ^ (value >> shift)
        shift //= 2
    return value & 1


def mix_kernel(nh, nl, count, rows_hbm, owner_hbm, signs_hbm, current_ref, gram_ref, sketch_ref,
               rows_ref, owner_ref, signs_ref, note_ref, notes, places, xbuf, ybuf, share, pair_in, chip_in, gathered,
               small_sem, load_sem, place_sem, nsend, nrecv, psend, precv, csend, crecv,
               gcsend, gcrecv, gpsend, gprecv):
    hi, lo = lax.axis_index("hi"), lax.axis_index("lo")
    bh, bl = bits_of(nh), bits_of(nl)
    devices = nh * nl
    rows, width = current_ref.shape
    total = devices * count
    loads = rows // TILE
    fars, mids = nl // 2, nh
    chips, group, half = fars * mids, mids * count, total // 2

    def masks(p):
        return (((p >> 1) & (nh // 2 - 1)) << 1 | (p >> (bl + bh - 1)),
                ((p >> bh) & (fars - 1)) << 1 | (p & 1))

    def peer(p):
        mask_hi, mask_lo = masks(p)
        return (hi ^ mask_hi, lo ^ mask_lo)

    def load(c):
        at = pl.ds(c * TILE, TILE)
        return pltpu.make_async_copy(current_ref.at[at, :], xbuf.at[at, :], load_sem.at[c])

    small = [pltpu.make_async_copy(source, target, small_sem.at[k])
             for k, (source, target) in enumerate(
                 ((rows_hbm, rows_ref), (owner_hbm, owner_ref), (signs_hbm, signs_ref)))]
    for copy in small:
        copy.start()
    barrier = pltpu.get_barrier_semaphore()
    for p in range(1, devices):
        pl.semaphore_signal(barrier, inc=1, device_id=peer(p), device_id_type=MESH)
    for c in range(loads):
        load(c).start()
    for copy in small:
        copy.wait()
    note_ref[...] = jnp.zeros_like(note_ref)
    note_ref[:, 0:count] = rows_ref[...]
    note_ref[:, count:2 * count] = owner_ref[...]

    up = lax.broadcasted_iota(jnp.int32, (TILE, TILE), 0)
    across = lax.broadcasted_iota(jnp.int32, (TILE, TILE), 1)
    table = (1 - 2 * parity(up & across, TILE)).astype(F32).astype(BF16)

    def transform(first, last):
        for c in range(first, last):
            load(c).wait()
        for c in range(first, last):
            at = slice(c * TILE, (c + 1) * TILE)
            lanes = TILE // LANES
            sign = jnp.concatenate([signs_ref[c * lanes + k:c * lanes + k + 1, :] for k in range(lanes)], axis=1)
            signed = table * sign.astype(F32).astype(BF16)
            x = xbuf[at, :]
            top = x.astype(BF16)
            rest = (x - top.astype(F32)).astype(BF16)
            ybuf[at, :] = jnp.dot(jnp.concatenate([signed, signed], axis=1), jnp.concatenate([top, rest], axis=0),
                                  preferred_element_type=F32)

    transform(0, loads // 2)
    transform(loads // 2, loads)
    pl.semaphore_wait(barrier, devices - 1)

    def note(p):
        return pltpu.make_async_remote_copy(
            src_ref=note_ref, dst_ref=notes.at[pl.ds(p, 1), :],
            send_sem=nsend.at[p], recv_sem=nrecv.at[p],
            device_id=peer(p), device_id_type=MESH)

    for p in reversed(range(1, devices)):
        note(p).start()
    notes[0:1, :] = note_ref[...]

    @pl.loop(0, TILE // 8)
    def _(r):
        first = pl.multiple_of(r * 8, 8)
        block = [ybuf[pl.ds(first + c * TILE, 8), :] for c in range(loads)]
        step = 1
        while step < loads:
            block = [block[c] + block[c + step] if not c & step else block[c - step] - block[c]
                     for c in range(loads)]
            step *= 2
        for c in range(loads):
            xbuf[pl.ds(first + c * TILE, 8), :] = block[c]

    for p in range(1, devices):
        note(p).wait_recv()
    spread = pltpu.make_async_copy(notes, places, place_sem)
    spread.start()
    spread.wait()

    def pick(first, size):
        @pl.loop(first // count, (first + size) // count, unroll=2)
        def _(p):
            mask_hi, mask_lo = masks(p)
            odd = parity(((hi & ~mask_hi) << bl) | (lo & ~mask_lo), devices)
            flip = (1 - 2 * odd).astype(F32)
            base = pl.multiple_of(p * count, count)
            for i in range(count):
                share[pl.ds(base + i, 1), :] = xbuf[pl.ds(places[p, i], 1), :] * flip

    def sketch_tables():
        span = nl * count
        owners = jnp.concatenate([notes[q * mids:q * mids + 2, :] for q in range(fars)], axis=0)
        k = lax.broadcasted_iota(jnp.int32, (nl, LANES), 1)
        mine = (owners == lo) & (k >= count) & (k < 2 * count)
        match = jnp.where(mine, 1.0, 0.0).astype(F32)
        up = lax.broadcasted_iota(jnp.int32, (LANES, LANES), 0)
        across = lax.broadcasted_iota(jnp.int32, (LANES, LANES), 1)
        ahead = jnp.where(up < across, 1.0, 0.0).astype(F32)
        before = jnp.dot(match, ahead, precision=HIGHEST, preferred_element_type=F32)
        spread_row = lax.broadcasted_iota(jnp.int32, (LANES, span), 0)
        spread_col = lax.broadcasted_iota(jnp.int32, (LANES, span), 1)
        spread = jnp.where(spread_row - count == spread_col % count, 1.0, 0.0).astype(F32)
        lead = lax.broadcasted_iota(jnp.int32, (nl, span), 0)
        cell = lax.broadcasted_iota(jnp.int32, (nl, span), 1)
        order_row = lax.broadcasted_iota(jnp.int32, (nl, nl), 0)
        order_col = lax.broadcasted_iota(jnp.int32, (nl, nl), 1)
        turn = jnp.where((order_col ^ lo) == order_row, 1.0, 0.0).astype(F32)
        made = []
        for m in range(MOST):
            chosen = jnp.where(jnp.abs(before - m) < 0.5, match, 0.0)
            wide = jnp.dot(chosen, spread, precision=HIGHEST, preferred_element_type=F32)
            wide = jnp.where(cell // count == lead, wide, 0.0)
            made.append(jnp.dot(turn, wide, precision=HIGHEST, preferred_element_type=F32))
        return made

    def remote(source, target, send, recv, p):
        return pltpu.make_async_remote_copy(src_ref=source, dst_ref=target, send_sem=send, recv_sem=recv,
                                            device_id=peer(p), device_id_type=MESH)

    pair = devices // 2

    def block(ref, p):
        return ref.at[pl.ds(p * count, count), :]

    def groups(ref, q):
        return ref.at[pl.ds(q * group, group), :]

    def pair_sum(q):
        return remote(groups(share, fars + q), groups(pair_in, q), psend.at[q], precv.at[q], pair)

    def chip_sum(p):
        return remote(block(share, p), block(chip_in, p), csend.at[p], crecv.at[p], p)

    def chip_gather(p):
        return remote(block(gathered, 0), block(gathered, p), gcsend.at[p], gcrecv.at[p], p)

    def pair_gather(q):
        return remote(groups(gathered, q), groups(gathered, fars + q), gpsend.at[q], gprecv.at[q], pair)

    for q in reversed(range(fars)):
        pick(half + q * group, group)
        pair_sum(q).start()
    for q in reversed(range(fars)):
        pick(q * group, group)
        pair_sum(q).wait_recv()
        at = slice(q * group, (q + 1) * group)
        share[at, :] = share[at, :] + pair_in[at, :]
        for p in reversed(range(max(q * mids, 1), (q + 1) * mids)):
            chip_sum(p).start()
    tables = sketch_tables()
    kept = share[0:count, :]
    for p in range(1, chips):
        chip_sum(p).wait_recv()
        kept = kept + chip_in[p * count:(p + 1) * count, :]
    gathered[0:count, :] = kept * (1.0 / math.sqrt(rows * devices))
    for p in reversed(range(1, chips)):
        chip_gather(p).start()

    def product(first, size):
        top, mid, low = three(gathered[first:first + size, :])
        left = jnp.concatenate([top, top, mid, top, low, mid], axis=0)
        right = jnp.concatenate([top, mid, top, low, top, mid], axis=0)
        return lax.dot_general(left, right, (((0,), (0,)), ((), ())), preferred_element_type=F32)

    gram = 0.0
    for q in range(fars):
        for p in range(max(q * mids, 1), (q + 1) * mids):
            chip_gather(p).wait_recv()
        pair_gather(q).start()
        gram = gram + product(q * group, group)

    rows_here = jnp.concatenate([gathered[q * group:q * group + 2 * count, :] for q in range(fars)], axis=0)
    for m in range(MOST):
        sketch_ref[m, :, :] = jnp.dot(tables[m], rows_here, precision=HIGHEST, preferred_element_type=F32)
    for q in range(fars):
        pair_gather(q).wait_recv()
        gram = gram + product(half + q * group, group)
    gram_ref[...] = gram * (1.0 / total)

    for p in range(1, devices):
        note(p).wait_send()
    for q in range(fars):
        pair_sum(q).wait_send()
        pair_gather(q).wait_send()
    for p in range(1, chips):
        chip_sum(p).wait_send()
        chip_gather(p).wait_send()


def eliminate(both, hook):
    nb = both.shape[0]
    sub = lax.broadcasted_iota(jnp.int32, (8, both.shape[1]), 0)
    wide = (8, both.shape[1])
    tiles = [both[8 * g:8 * g + 8, :] for g in range(nb // 8)]
    for g0 in range(nb // 8):
        hook()
        cols = {}
        for g in range(g0, nb // 8):
            cols[g] = [jnp.broadcast_to(tiles[g][:, 8 * g0 + j:8 * g0 + j + 1], wide) for j in range(8)]
        for i in range(8):
            if i == 7 and g0 == nb // 8 - 1:
                break
            lead = cols[g0]
            flip = 1.0 / lead[i][i:i + 1, :]
            pivot = tiles[g0][i:i + 1, :]
            heads = [lead[j][i:i + 1, :] for j in range(8)]
            for g in range(g0, nb // 8):
                if g == g0 and i == 7:
                    continue
                rate = cols[g][i] * flip
                if g == g0:
                    rate = jnp.where(sub > i, rate, 0.0)
                for j in range(i + 1, 8):
                    cols[g][j] = cols[g][j] - rate * heads[j]
                tiles[g] = tiles[g] - rate * pivot
    return jnp.concatenate(tiles, axis=0)


def three(value):
    top = value.astype(BF16)
    value = value - top.astype(F32)
    mid = value.astype(BF16)
    return top, mid, (value - mid.astype(F32)).astype(BF16)


def factor_kernel(gram_ref, sketch_in, current_ref, sketch_ref, r_ref, out_ref,
                  xbuf, parts, obuf, load_sem, store_sem):
    rows, width = current_ref.shape
    blocks = width // BLOCK
    turns = width // 32
    pieces = turns
    step = rows // pieces
    wide = width // 2

    def load(c):
        at = pl.ds(c * step, step)
        return pltpu.make_async_copy(current_ref.at[at, :], xbuf.at[at, :], load_sem.at[c])

    def store(c, side):
        at = (pl.ds(c * step, step), pl.ds(side * wide, wide))
        return pltpu.make_async_copy(obuf.at[at], out_ref.at[at], store_sem.at[c, side])

    for c in range(pieces):
        load(c).start()
    for source in range(sketch_ref.shape[0]):
        for m in range(MOST):
            sketch_ref[source, m:m + 1, :] = sketch_in[m, source:source + 1, :]

    def split(c):
        load(c).wait()
        at = slice(c * step, (c + 1) * step)
        x = xbuf[at, :]
        top = x.astype(BF16)
        rest = (x - top.astype(F32)).astype(BF16)
        parts[at, 0:wide] = top[:, 0:wide]
        parts[at, wide:2 * wide] = rest[:, 0:wide]
        parts[at, 2 * wide:3 * wide] = top[:, wide:]
        parts[at, 3 * wide:] = rest[:, wide:]

    def turned(inverse):
        inverse = inverse.T
        top = inverse.astype(BF16)
        rest = (inverse - top.astype(F32)).astype(BF16)
        both = jnp.concatenate([top, rest], axis=1)
        return jnp.concatenate([both[k * wide:(k + 1) * wide, :]
                                for k in range(both.shape[0] // wide) for _ in range(2)], axis=0)

    def solve(first, last, stack, side):
        x = parts[first:last, 0:stack.shape[0]]
        both = jnp.dot(x, stack, preferred_element_type=F32)
        obuf[first:last, side * wide:(side + 1) * wide] = both[:, 0:wide] + both[:, wide:]

    state = {"turn": 0, "stack": None}

    def hook():
        turn = state["turn"]
        state["turn"] += 1
        if turns <= turn < 2 * turns:
            split(turn - turns)
        elif turn >= 2 * turns:
            turn -= 2 * turns
            half = step // 2
            solve(turn * half, (turn + 1) * half, state["stack"], 0)
            if turn % 2:
                store(turn // 2, 0).start()

    size = (BLOCK, LANES)
    row = lax.broadcasted_iota(jnp.int32, size, 0)
    lane = lax.broadcasted_iota(jnp.int32, size, 1)
    halves = range(width // LANES)
    left_half = lane < BLOCK
    unit = jnp.where(row == lane - BLOCK, 1.0, 0.0).astype(F32)
    a = [[gram_ref[k * BLOCK:(k + 1) * BLOCK, h * LANES:(h + 1) * LANES] for h in halves] for k in range(blocks)]
    inverse = []
    for k in range(blocks):
        first, last = k * BLOCK, (k + 1) * BLOCK
        if k == blocks // 2:
            state["stack"] = turned(jnp.concatenate(inverse, axis=0)[:, 0:wide])
        home, start = first // LANES, first % LANES
        own = a[k][home]
        if start:
            own = pltpu.roll(own, BLOCK, 1)
        both = eliminate(jnp.where(left_half, own, unit), hook)
        diag = jnp.sum(jnp.where(row == lane, both, 0.0), axis=1, keepdims=True)
        both = both * (1.0 / jnp.sqrt(diag))
        both = jnp.where(left_half, pltpu.roll(both, BLOCK, 1), both)
        top, mid, low = [part.astype(F32) for part in three(both)]
        left = jnp.concatenate([top, jnp.where(left_half, top, mid), jnp.where(left_half, mid, low)], axis=1).astype(BF16)
        top, mid, low = three(jnp.concatenate(a[k], axis=1))
        right = jnp.concatenate([top, mid, low, top, mid, top], axis=0)
        done = jnp.dot(left, right, preferred_element_type=F32)
        done = [done[:, h * LANES:(h + 1) * LANES] for h in halves]
        for h in halves:
            r_ref[first:last, h * LANES:(h + 1) * LANES] = jnp.where(row + first <= lane + h * LANES, done[h], 0.0)
        inside = (lane >= start) & (lane < start + BLOCK)
        done[home] = jnp.where(inside, both, done[home])
        inverse.append(jnp.concatenate([jnp.where(lane + h * LANES < last, done[h], 0.0) for h in halves], axis=1))
        if k == blocks - 1:
            break
        top, mid, low = three(jnp.concatenate(done, axis=1))
        base = last // LANES * LANES
        left = jnp.concatenate([top, top, mid, top, low, mid], axis=0)
        right = jnp.concatenate([top, mid, top, low, top, mid], axis=0)
        for part in range(base, width, LANES):
            change = lax.dot_general(left[:, part:part + LANES], right, (((0,), (0,)), ((), ())),
                                     preferred_element_type=F32)
            for later in range(max(k + 1, part // BLOCK), (part + LANES) // BLOCK):
                at = later * BLOCK - part
                for h in halves:
                    old = jnp.where(inside, 0.0, a[later][h]) if h == home else a[later][h]
                    a[later][h] = old - change[at:at + BLOCK, h * LANES:(h + 1) * LANES]
    stack = turned(jnp.concatenate(inverse[blocks // 2:], axis=0))
    for c in range(pieces):
        solve(c * step, (c + 1) * step, stack, 1)
        store(c, 1).start()
    for c in range(pieces):
        store(c, 0).wait()
        store(c, 1).wait()


def shards(nh, nl, current, signs, sample_rows, sample_owner):
    rows, width = current.shape
    count = sample_rows.shape[0]
    devices = nh * nl
    total = devices * count
    vmem = pl.BlockSpec(memory_space=pltpu.VMEM)
    anywhere = pl.BlockSpec(memory_space=pl.ANY)
    dma = pltpu.SemaphoreType.DMA
    gram, picked = pl.pallas_call(
        functools.partial(mix_kernel, nh, nl, count),
        name="mix",
        out_shape=(jax.ShapeDtypeStruct((width, width), F32),
                   jax.ShapeDtypeStruct((MOST, nl, width), F32)),
        in_specs=[anywhere, anywhere, anywhere, anywhere],
        out_specs=(vmem, vmem),
        scratch_shapes=[
            pltpu.VMEM((1, count), jnp.int32),
            pltpu.VMEM((1, count), jnp.int32),
            pltpu.VMEM((rows // LANES, LANES), jnp.int32),
            pltpu.VMEM((1, LANES), jnp.int32),
            pltpu.VMEM((devices, LANES), jnp.int32),
            pltpu.SMEM((devices, LANES), jnp.int32),
            pltpu.VMEM((rows, width), F32),
            pltpu.VMEM((rows, width), F32),
            pltpu.VMEM((total, width), F32),
            pltpu.VMEM((total // 2, width), F32),
            pltpu.VMEM((total // 2, width), F32),
            pltpu.VMEM((total, width), F32),
            dma((3,)), dma((rows // TILE,)), dma, dma((devices,)), dma((devices,)),
            dma((nl // 2,)), dma((nl // 2,)), dma((devices // 2,)), dma((devices // 2,)),
            dma((devices // 2,)), dma((devices // 2,)), dma((nl // 2,)), dma((nl // 2,)),
        ],
        compiler_params=pltpu.CompilerParams(
            collective_id=0, has_side_effects=True, vmem_limit_bytes=VMEM_LIMIT),
    )(sample_rows.reshape(1, count), sample_owner.reshape(1, count), signs.reshape(rows // LANES, LANES), current)
    sketch, r_factor, precond = pl.pallas_call(
        factor_kernel,
        name="factor",
        out_shape=(jax.ShapeDtypeStruct((nl, MOST, width), F32),
                   jax.ShapeDtypeStruct((width, width), F32),
                   jax.ShapeDtypeStruct((rows, width), F32)),
        in_specs=[vmem, vmem, anywhere],
        out_specs=(vmem, vmem, anywhere),
        scratch_shapes=[
            pltpu.VMEM((rows, width), F32),
            pltpu.VMEM((rows, 2 * width), BF16),
            pltpu.VMEM((rows, width), F32),
            dma((width // 32,)), dma((width // 32, 2)),
        ],
        compiler_params=pltpu.CompilerParams(vmem_limit_bytes=VMEM_LIMIT),
    )(gram, picked, current)
    return (sketch.reshape(1, 1, nl, MOST, width), r_factor, precond)


def solution(mesh):
    placed = (P(("hi", "lo"), None), P(("hi", "lo")), P(("hi", "lo")), P(("hi", "lo"), None))
    return jax.shard_map(
        functools.partial(shards, mesh.shape["hi"], mesh.shape["lo"]),
        mesh=mesh,
        in_specs=placed,
        out_specs=(P("hi", "lo", None, None, None), P(), P(("hi", "lo"), None)),
        check_vma=False,
    )
```

```python
import functools
import math

import jax
import jax.numpy as jnp
from jax import lax
from jax.experimental import pallas as pl
from jax.experimental.pallas import tpu as pltpu
from jax.sharding import PartitionSpec as P

MOST = 2
LANES = 128
BLOCK = 64
TILE = 256
VMEM_LIMIT = 61 * 2 ** 20
MESH = pl.DeviceIdType.MESH
HIGHEST = lax.Precision.HIGHEST
F32 = jnp.float32
BF16 = jnp.bfloat16


def bits_of(size):
    return size.bit_length() - 1


def parity(value, top):
    shift = 1
    while shift * 2 < top:
        shift *= 2
    while shift >= 1:
        value = value ^ (value >> shift)
        shift //= 2
    return value & 1


def mix_kernel(nh, nl, count, rows_hbm, owner_hbm, signs_hbm, current_ref, gram_ref, sketch_ref,
               rows_ref, owner_ref, signs_ref, note_ref, notes, places, xbuf, ybuf, share, pair_in, chip_in, gathered,
               small_sem, load_sem, place_sem, nsend, nrecv, psend, precv, csend, crecv,
               gcsend, gcrecv, gpsend, gprecv):
    hi, lo = lax.axis_index("hi"), lax.axis_index("lo")
    bh, bl = bits_of(nh), bits_of(nl)
    devices = nh * nl
    rows, width = current_ref.shape
    total = devices * count
    loads = rows // TILE
    fars, mids = nl // 2, nh
    chips, group, half = fars * mids, mids * count, total // 2

    def masks(p):
        return (((p >> 1) & (nh // 2 - 1)) << 1 | (p >> (bl + bh - 1)),
                ((p >> bh) & (fars - 1)) << 1 | (p & 1))

    def peer(p):
        mask_hi, mask_lo = masks(p)
        return (hi ^ mask_hi, lo ^ mask_lo)

    def load(c):
        at = pl.ds(c * TILE, TILE)
        return pltpu.make_async_copy(current_ref.at[at, :], xbuf.at[at, :], load_sem.at[c])

    small = [pltpu.make_async_copy(source, target, small_sem.at[k])
             for k, (source, target) in enumerate(
                 ((rows_hbm, rows_ref), (owner_hbm, owner_ref), (signs_hbm, signs_ref)))]
    for copy in small:
        copy.start()
    barrier = pltpu.get_barrier_semaphore()
    for p in range(1, devices):
        pl.semaphore_signal(barrier, inc=1, device_id=peer(p), device_id_type=MESH)
    for c in range(loads):
        load(c).start()
    for copy in small:
        copy.wait()
    note_ref[...] = jnp.zeros_like(note_ref)
    note_ref[:, 0:count] = rows_ref[...]
    note_ref[:, count:2 * count] = owner_ref[...]

    up = lax.broadcasted_iota(jnp.int32, (TILE, TILE), 0)
    across = lax.broadcasted_iota(jnp.int32, (TILE, TILE), 1)
    table = (1 - 2 * parity(up & across, TILE)).astype(F32).astype(BF16)

    def transform(first, last):
        for c in range(first, last):
            load(c).wait()
        for c in range(first, last):
            at = slice(c * TILE, (c + 1) * TILE)
            lanes = TILE // LANES
            sign = jnp.concatenate([signs_ref[c * lanes + k:c * lanes + k + 1, :] for k in range(lanes)], axis=1)
            signed = table * sign.astype(F32).astype(BF16)
            x = xbuf[at, :]
            top = x.astype(BF16)
            rest = (x - top.astype(F32)).astype(BF16)
            ybuf[at, :] = jnp.dot(jnp.concatenate([signed, signed], axis=1), jnp.concatenate([top, rest], axis=0),
                                  preferred_element_type=F32)

    transform(0, loads // 2)
    transform(loads // 2, loads)
    pl.semaphore_wait(barrier, devices - 1)

    def note(p):
        return pltpu.make_async_remote_copy(
            src_ref=note_ref, dst_ref=notes.at[pl.ds(p, 1), :],
            send_sem=nsend.at[p], recv_sem=nrecv.at[p],
            device_id=peer(p), device_id_type=MESH)

    for p in reversed(range(1, devices)):
        note(p).start()
    notes[0:1, :] = note_ref[...]

    @pl.loop(0, TILE // 8)
    def _(r):
        first = pl.multiple_of(r * 8, 8)
        block = [ybuf[pl.ds(first + c * TILE, 8), :] for c in range(loads)]
        step = 1
        while step < loads:
            block = [block[c] + block[c + step] if not c & step else block[c - step] - block[c]
                     for c in range(loads)]
            step *= 2
        for c in range(loads):
            xbuf[pl.ds(first + c * TILE, 8), :] = block[c]

    for p in range(1, devices):
        note(p).wait_recv()
    spread = pltpu.make_async_copy(notes, places, place_sem)
    spread.start()
    spread.wait()

    def pick(first, size):
        @pl.loop(first // count, (first + size) // count, unroll=2)
        def _(p):
            mask_hi, mask_lo = masks(p)
            odd = parity(((hi & ~mask_hi) << bl) | (lo & ~mask_lo), devices)
            flip = (1 - 2 * odd).astype(F32)
            base = pl.multiple_of(p * count, count)
            for i in range(count):
                share[pl.ds(base + i, 1), :] = xbuf[pl.ds(places[p, i], 1), :] * flip

    def sketch_tables():
        span = nl * count
        owners = jnp.concatenate([notes[q * mids:q * mids + 2, :] for q in range(fars)], axis=0)
        k = lax.broadcasted_iota(jnp.int32, (nl, LANES), 1)
        mine = (owners == lo) & (k >= count) & (k < 2 * count)
        match = jnp.where(mine, 1.0, 0.0).astype(F32)
        up = lax.broadcasted_iota(jnp.int32, (LANES, LANES), 0)
        across = lax.broadcasted_iota(jnp.int32, (LANES, LANES), 1)
        ahead = jnp.where(up < across, 1.0, 0.0).astype(F32)
        before = jnp.dot(match, ahead, precision=HIGHEST, preferred_element_type=F32)
        spread_row = lax.broadcasted_iota(jnp.int32, (LANES, span), 0)
        spread_col = lax.broadcasted_iota(jnp.int32, (LANES, span), 1)
        spread = jnp.where(spread_row - count == spread_col % count, 1.0, 0.0).astype(F32)
        lead = lax.broadcasted_iota(jnp.int32, (nl, span), 0)
        cell = lax.broadcasted_iota(jnp.int32, (nl, span), 1)
        order_row = lax.broadcasted_iota(jnp.int32, (nl, nl), 0)
        order_col = lax.broadcasted_iota(jnp.int32, (nl, nl), 1)
        turn = jnp.where((order_col ^ lo) == order_row, 1.0, 0.0).astype(F32)
        made = []
        for m in range(MOST):
            chosen = jnp.where(jnp.abs(before - m) < 0.5, match, 0.0)
            wide = jnp.dot(chosen, spread, precision=HIGHEST, preferred_element_type=F32)
            wide = jnp.where(cell // count == lead, wide, 0.0)
            made.append(jnp.dot(turn, wide, precision=HIGHEST, preferred_element_type=F32))
        return made

    def remote(source, target, send, recv, p):
        return pltpu.make_async_remote_copy(src_ref=source, dst_ref=target, send_sem=send, recv_sem=recv,
                                            device_id=peer(p), device_id_type=MESH)

    pair = devices // 2

    def block(ref, p):
        return ref.at[pl.ds(p * count, count), :]

    def groups(ref, q):
        return ref.at[pl.ds(q * group, group), :]

    def pair_sum(q):
        return remote(groups(share, fars + q), groups(pair_in, q), psend.at[q], precv.at[q], pair)

    def chip_sum(p):
        return remote(block(share, p), block(chip_in, p), csend.at[p], crecv.at[p], p)

    def chip_gather(p):
        return remote(block(gathered, 0), block(gathered, p), gcsend.at[p], gcrecv.at[p], p)

    def pair_gather(q):
        return remote(groups(gathered, q), groups(gathered, fars + q), gpsend.at[q], gprecv.at[q], pair)

    for q in reversed(range(fars)):
        pick(half + q * group, group)
        pair_sum(q).start()
    for q in reversed(range(fars)):
        pick(q * group, group)
        pair_sum(q).wait_recv()
        at = slice(q * group, (q + 1) * group)
        share[at, :] = share[at, :] + pair_in[at, :]
        for p in reversed(range(max(q * mids, 1), (q + 1) * mids)):
            chip_sum(p).start()
    tables = sketch_tables()
    kept = share[0:count, :]
    for p in range(1, chips):
        chip_sum(p).wait_recv()
        kept = kept + chip_in[p * count:(p + 1) * count, :]
    gathered[0:count, :] = kept * (1.0 / math.sqrt(rows * devices))
    for p in reversed(range(1, chips)):
        chip_gather(p).start()

    def product(first, size):
        top, mid, low = three(gathered[first:first + size, :])
        left = jnp.concatenate([top, top, mid, top, low, mid], axis=0)
        right = jnp.concatenate([top, mid, top, low, top, mid], axis=0)
        return lax.dot_general(left, right, (((0,), (0,)), ((), ())), preferred_element_type=F32)

    gram = 0.0
    for q in range(fars):
        for p in range(max(q * mids, 1), (q + 1) * mids):
            chip_gather(p).wait_recv()
        pair_gather(q).start()
        gram = gram + product(q * group, group)

    rows_here = jnp.concatenate([gathered[q * group:q * group + 2 * count, :] for q in range(fars)], axis=0)
    top, mid, low = three(rows_here)
    table = jnp.concatenate(tables, axis=0).astype(BF16)
    picked = jnp.dot(jnp.concatenate([table, table, table], axis=1), jnp.concatenate([top, mid, low], axis=0),
                     preferred_element_type=F32)
    for m in range(MOST):
        sketch_ref[m, :, :] = picked[m * nl:(m + 1) * nl, :]
    for q in range(fars):
        pair_gather(q).wait_recv()
        gram = gram + product(half + q * group, group)
    gram_ref[...] = gram * (1.0 / total)

    for p in range(1, devices):
        note(p).wait_send()
    for q in range(fars):
        pair_sum(q).wait_send()
        pair_gather(q).wait_send()
    for p in range(1, chips):
        chip_sum(p).wait_send()
        chip_gather(p).wait_send()


def eliminate(both, hook):
    nb = both.shape[0]
    sub = lax.broadcasted_iota(jnp.int32, (8, both.shape[1]), 0)
    wide = (8, both.shape[1])
    tiles = [both[8 * g:8 * g + 8, :] for g in range(nb // 8)]
    for g0 in range(nb // 8):
        hook()
        cols = {}
        for g in range(g0, nb // 8):
            cols[g] = [jnp.broadcast_to(tiles[g][:, 8 * g0 + j:8 * g0 + j + 1], wide) for j in range(8)]
        for i in range(8):
            if i == 7 and g0 == nb // 8 - 1:
                break
            lead = cols[g0]
            flip = 1.0 / lead[i][i:i + 1, :]
            pivot = tiles[g0][i:i + 1, :]
            heads = [lead[j][i:i + 1, :] for j in range(8)]
            for g in range(g0, nb // 8):
                if g == g0 and i == 7:
                    continue
                rate = cols[g][i] * flip
                if g == g0:
                    rate = jnp.where(sub > i, rate, 0.0)
                for j in range(i + 1, 8):
                    cols[g][j] = cols[g][j] - rate * heads[j]
                tiles[g] = tiles[g] - rate * pivot
    return jnp.concatenate(tiles, axis=0)


def three(value):
    top = value.astype(BF16)
    value = value - top.astype(F32)
    mid = value.astype(BF16)
    return top, mid, (value - mid.astype(F32)).astype(BF16)


def factor_kernel(gram_ref, sketch_in, current_ref, sketch_ref, r_ref, out_ref,
                  xbuf, parts, obuf, load_sem, store_sem):
    rows, width = current_ref.shape
    blocks = width // BLOCK
    turns = width // 32
    pieces = turns
    step = rows // pieces
    wide = width // 2

    def load(c):
        at = pl.ds(c * step, step)
        return pltpu.make_async_copy(current_ref.at[at, :], xbuf.at[at, :], load_sem.at[c])

    def store(c, side):
        at = (pl.ds(c * step, step), pl.ds(side * wide, wide))
        return pltpu.make_async_copy(obuf.at[at], out_ref.at[at], store_sem.at[c, side])

    for c in range(pieces):
        load(c).start()
    for source in range(sketch_ref.shape[0]):
        for m in range(MOST):
            sketch_ref[source, m:m + 1, :] = sketch_in[m, source:source + 1, :]

    def split(c):
        load(c).wait()
        at = slice(c * step, (c + 1) * step)
        x = xbuf[at, :]
        top = x.astype(BF16)
        rest = (x - top.astype(F32)).astype(BF16)
        parts[at, 0:wide] = top[:, 0:wide]
        parts[at, wide:2 * wide] = rest[:, 0:wide]
        parts[at, 2 * wide:3 * wide] = top[:, wide:]
        parts[at, 3 * wide:] = rest[:, wide:]

    def turned(inverse):
        inverse = inverse.T
        top = inverse.astype(BF16)
        rest = (inverse - top.astype(F32)).astype(BF16)
        both = jnp.concatenate([top, rest], axis=1)
        return jnp.concatenate([both[k * wide:(k + 1) * wide, :]
                                for k in range(both.shape[0] // wide) for _ in range(2)], axis=0)

    def solve(first, last, stack, side):
        x = parts[first:last, 0:stack.shape[0]]
        both = jnp.dot(x, stack, preferred_element_type=F32)
        obuf[first:last, side * wide:(side + 1) * wide] = both[:, 0:wide] + both[:, wide:]

    state = {"turn": 0, "stack": None}

    def hook():
        turn = state["turn"]
        state["turn"] += 1
        if turns <= turn < 2 * turns:
            split(turn - turns)
        elif turn >= 2 * turns:
            turn -= 2 * turns
            half = step // 2
            solve(turn * half, (turn + 1) * half, state["stack"], 0)
            if turn % 2:
                store(turn // 2, 0).start()

    size = (BLOCK, LANES)
    row = lax.broadcasted_iota(jnp.int32, size, 0)
    lane = lax.broadcasted_iota(jnp.int32, size, 1)
    halves = range(width // LANES)
    left_half = lane < BLOCK
    unit = jnp.where(row == lane - BLOCK, 1.0, 0.0).astype(F32)
    a = [[gram_ref[k * BLOCK:(k + 1) * BLOCK, h * LANES:(h + 1) * LANES] for h in halves] for k in range(blocks)]
    inverse = []
    for k in range(blocks):
        first, last = k * BLOCK, (k + 1) * BLOCK
        if k == blocks // 2:
            state["stack"] = turned(jnp.concatenate(inverse, axis=0)[:, 0:wide])
        home, start = first // LANES, first % LANES
        own = a[k][home]
        if start:
            own = pltpu.roll(own, BLOCK, 1)
        both = eliminate(jnp.where(left_half, own, unit), hook)
        diag = jnp.sum(jnp.where(row == lane, both, 0.0), axis=1, keepdims=True)
        both = both * (1.0 / jnp.sqrt(diag))
        both = jnp.where(left_half, pltpu.roll(both, BLOCK, 1), both)
        top, mid, low = [part.astype(F32) for part in three(both)]
        left = jnp.concatenate([top, jnp.where(left_half, top, mid), jnp.where(left_half, mid, low)], axis=1).astype(BF16)
        top, mid, low = three(jnp.concatenate(a[k], axis=1))
        right = jnp.concatenate([top, mid, low, top, mid, top], axis=0)
        done = jnp.dot(left, right, preferred_element_type=F32)
        done = [done[:, h * LANES:(h + 1) * LANES] for h in halves]
        for h in halves:
            r_ref[first:last, h * LANES:(h + 1) * LANES] = jnp.where(row + first <= lane + h * LANES, done[h], 0.0)
        inside = (lane >= start) & (lane < start + BLOCK)
        done[home] = jnp.where(inside, both, done[home])
        inverse.append(jnp.concatenate([jnp.where(lane + h * LANES < last, done[h], 0.0) for h in halves], axis=1))
        if k == blocks - 1:
            break
        top, mid, low = three(jnp.concatenate(done, axis=1))
        base = last // LANES * LANES
        left = jnp.concatenate([top, top, mid, top, low, mid], axis=0)
        right = jnp.concatenate([top, mid, top, low, top, mid], axis=0)
        for part in range(base, width, LANES):
            change = lax.dot_general(left[:, part:part + LANES], right, (((0,), (0,)), ((), ())),
                                     preferred_element_type=F32)
            for later in range(max(k + 1, part // BLOCK), (part + LANES) // BLOCK):
                at = later * BLOCK - part
                for h in halves:
                    old = jnp.where(inside, 0.0, a[later][h]) if h == home else a[later][h]
                    a[later][h] = old - change[at:at + BLOCK, h * LANES:(h + 1) * LANES]
    stack = turned(jnp.concatenate(inverse[blocks // 2:], axis=0))
    for c in range(pieces):
        solve(c * step, (c + 1) * step, stack, 1)
        store(c, 1).start()
    for c in range(pieces):
        store(c, 0).wait()
        store(c, 1).wait()


def shards(nh, nl, current, signs, sample_rows, sample_owner):
    rows, width = current.shape
    count = sample_rows.shape[0]
    devices = nh * nl
    total = devices * count
    vmem = pl.BlockSpec(memory_space=pltpu.VMEM)
    anywhere = pl.BlockSpec(memory_space=pl.ANY)
    dma = pltpu.SemaphoreType.DMA
    gram, picked = pl.pallas_call(
        functools.partial(mix_kernel, nh, nl, count),
        name="mix",
        out_shape=(jax.ShapeDtypeStruct((width, width), F32),
                   jax.ShapeDtypeStruct((MOST, nl, width), F32)),
        in_specs=[anywhere, anywhere, anywhere, anywhere],
        out_specs=(vmem, vmem),
        scratch_shapes=[
            pltpu.VMEM((1, count), jnp.int32),
            pltpu.VMEM((1, count), jnp.int32),
            pltpu.VMEM((rows // LANES, LANES), jnp.int32),
            pltpu.VMEM((1, LANES), jnp.int32),
            pltpu.VMEM((devices, LANES), jnp.int32),
            pltpu.SMEM((devices, LANES), jnp.int32),
            pltpu.VMEM((rows, width), F32),
            pltpu.VMEM((rows, width), F32),
            pltpu.VMEM((total, width), F32),
            pltpu.VMEM((total // 2, width), F32),
            pltpu.VMEM((total // 2, width), F32),
            pltpu.VMEM((total, width), F32),
            dma((3,)), dma((rows // TILE,)), dma, dma((devices,)), dma((devices,)),
            dma((nl // 2,)), dma((nl // 2,)), dma((devices // 2,)), dma((devices // 2,)),
            dma((devices // 2,)), dma((devices // 2,)), dma((nl // 2,)), dma((nl // 2,)),
        ],
        compiler_params=pltpu.CompilerParams(
            collective_id=0, has_side_effects=True, vmem_limit_bytes=VMEM_LIMIT),
    )(sample_rows.reshape(1, count), sample_owner.reshape(1, count), signs.reshape(rows // LANES, LANES), current)
    sketch, r_factor, precond = pl.pallas_call(
        factor_kernel,
        name="factor",
        out_shape=(jax.ShapeDtypeStruct((nl, MOST, width), F32),
                   jax.ShapeDtypeStruct((width, width), F32),
                   jax.ShapeDtypeStruct((rows, width), F32)),
        in_specs=[vmem, vmem, anywhere],
        out_specs=(vmem, vmem, anywhere),
        scratch_shapes=[
            pltpu.VMEM((rows, width), F32),
            pltpu.VMEM((rows, 2 * width), BF16),
            pltpu.VMEM((rows, width), F32),
            dma((width // 32,)), dma((width // 32, 2)),
        ],
        compiler_params=pltpu.CompilerParams(vmem_limit_bytes=VMEM_LIMIT),
    )(gram, picked, current)
    return (sketch.reshape(1, 1, nl, MOST, width), r_factor, precond)


def solution(mesh):
    placed = (P(("hi", "lo"), None), P(("hi", "lo")), P(("hi", "lo")), P(("hi", "lo"), None))
    return jax.shard_map(
        functools.partial(shards, mesh.shape["hi"], mesh.shape["lo"]),
        mesh=mesh,
        in_specs=placed,
        out_specs=(P("hi", "lo", None, None, None), P(), P(("hi", "lo"), None)),
        check_vma=False,
    )
```

```python
import functools
import math

import jax
import jax.numpy as jnp
from jax import lax
from jax.experimental import pallas as pl
from jax.experimental.pallas import tpu as pltpu
from jax.sharding import PartitionSpec as P

MOST = 2
LANES = 128
BLOCK = 64
TILE = 256
VMEM_LIMIT = 61 * 2 ** 20
MESH = pl.DeviceIdType.MESH
HIGHEST = lax.Precision.HIGHEST
F32 = jnp.float32
BF16 = jnp.bfloat16


def bits_of(size):
    return size.bit_length() - 1


def parity(value, top):
    shift = 1
    while shift * 2 < top:
        shift *= 2
    while shift >= 1:
        value = value ^ (value >> shift)
        shift //= 2
    return value & 1


def mix_kernel(nh, nl, count, rows_hbm, owner_hbm, signs_hbm, current_ref, gram_ref, sketch_ref,
               rows_ref, owner_ref, signs_ref, note_ref, notes, places, xbuf, ybuf, share, pair_in, chip_in, gathered,
               small_sem, load_sem, place_sem, nsend, nrecv, psend, precv, csend, crecv,
               gcsend, gcrecv, gpsend, gprecv):
    hi, lo = lax.axis_index("hi"), lax.axis_index("lo")
    bh, bl = bits_of(nh), bits_of(nl)
    devices = nh * nl
    rows, width = current_ref.shape
    total = devices * count
    loads = rows // TILE
    fars, mids = nl // 2, nh
    chips, group, half = fars * mids, mids * count, total // 2

    def masks(p):
        return (((p >> 1) & (nh // 2 - 1)) << 1 | (p >> (bl + bh - 1)),
                ((p >> bh) & (fars - 1)) << 1 | (p & 1))

    def peer(p):
        mask_hi, mask_lo = masks(p)
        return (hi ^ mask_hi, lo ^ mask_lo)

    def load(c):
        at = pl.ds(c * TILE, TILE)
        return pltpu.make_async_copy(current_ref.at[at, :], xbuf.at[at, :], load_sem.at[c])

    small = [pltpu.make_async_copy(source, target, small_sem.at[k])
             for k, (source, target) in enumerate(
                 ((rows_hbm, rows_ref), (owner_hbm, owner_ref), (signs_hbm, signs_ref)))]
    for copy in small:
        copy.start()
    barrier = pltpu.get_barrier_semaphore()
    for p in range(1, devices):
        pl.semaphore_signal(barrier, inc=1, device_id=peer(p), device_id_type=MESH)
    for c in range(loads):
        load(c).start()
    for copy in small:
        copy.wait()
    note_ref[...] = jnp.zeros_like(note_ref)
    note_ref[:, 0:count] = rows_ref[...]
    note_ref[:, count:2 * count] = owner_ref[...]

    up = lax.broadcasted_iota(jnp.int32, (TILE, TILE), 0)
    across = lax.broadcasted_iota(jnp.int32, (TILE, TILE), 1)
    table = (1 - 2 * parity(up & across, TILE)).astype(F32).astype(BF16)

    def transform(first, last):
        for c in range(first, last):
            load(c).wait()
        for c in range(first, last):
            at = slice(c * TILE, (c + 1) * TILE)
            lanes = TILE // LANES
            sign = jnp.concatenate([signs_ref[c * lanes + k:c * lanes + k + 1, :] for k in range(lanes)], axis=1)
            signed = table * sign.astype(F32).astype(BF16)
            x = xbuf[at, :]
            top = x.astype(BF16)
            rest = (x - top.astype(F32)).astype(BF16)
            ybuf[at, :] = jnp.dot(jnp.concatenate([signed, signed], axis=1), jnp.concatenate([top, rest], axis=0),
                                  preferred_element_type=F32)

    transform(0, loads // 2)
    transform(loads // 2, loads)
    pl.semaphore_wait(barrier, devices - 1)

    def note(p):
        return pltpu.make_async_remote_copy(
            src_ref=note_ref, dst_ref=notes.at[pl.ds(p, 1), :],
            send_sem=nsend.at[p], recv_sem=nrecv.at[p],
            device_id=peer(p), device_id_type=MESH)

    for p in sorted(range(1, devices), key=lambda p: -(p % chips)):
        note(p).start()
    notes[0:1, :] = note_ref[...]

    @pl.loop(0, TILE // 8)
    def _(r):
        first = pl.multiple_of(r * 8, 8)
        block = [ybuf[pl.ds(first + c * TILE, 8), :] for c in range(loads)]
        step = 1
        while step < loads:
            block = [block[c] + block[c + step] if not c & step else block[c - step] - block[c]
                     for c in range(loads)]
            step *= 2
        for c in range(loads):
            xbuf[pl.ds(first + c * TILE, 8), :] = block[c]

    for p in range(1, devices):
        note(p).wait_recv()
    spread = pltpu.make_async_copy(notes, places, place_sem)
    spread.start()
    spread.wait()

    def pick(first, size):
        @pl.loop(first // count, (first + size) // count, unroll=2)
        def _(p):
            mask_hi, mask_lo = masks(p)
            odd = parity(((hi & ~mask_hi) << bl) | (lo & ~mask_lo), devices)
            flip = (1 - 2 * odd).astype(F32)
            base = pl.multiple_of(p * count, count)
            for i in range(count):
                share[pl.ds(base + i, 1), :] = xbuf[pl.ds(places[p, i], 1), :] * flip

    def sketch_tables():
        span = nl * count
        owners = jnp.concatenate([notes[q * mids:q * mids + 2, :] for q in range(fars)], axis=0)
        k = lax.broadcasted_iota(jnp.int32, (nl, LANES), 1)
        mine = (owners == lo) & (k >= count) & (k < 2 * count)
        match = jnp.where(mine, 1.0, 0.0).astype(F32)
        up = lax.broadcasted_iota(jnp.int32, (LANES, LANES), 0)
        across = lax.broadcasted_iota(jnp.int32, (LANES, LANES), 1)
        ahead = jnp.where(up < across, 1.0, 0.0).astype(F32)
        before = jnp.dot(match, ahead, precision=HIGHEST, preferred_element_type=F32)
        spread_row = lax.broadcasted_iota(jnp.int32, (LANES, span), 0)
        spread_col = lax.broadcasted_iota(jnp.int32, (LANES, span), 1)
        spread = jnp.where(spread_row - count == spread_col % count, 1.0, 0.0).astype(F32)
        lead = lax.broadcasted_iota(jnp.int32, (nl, span), 0)
        cell = lax.broadcasted_iota(jnp.int32, (nl, span), 1)
        order_row = lax.broadcasted_iota(jnp.int32, (nl, nl), 0)
        order_col = lax.broadcasted_iota(jnp.int32, (nl, nl), 1)
        turn = jnp.where((order_col ^ lo) == order_row, 1.0, 0.0).astype(F32)
        made = []
        for m in range(MOST):
            chosen = jnp.where(jnp.abs(before - m) < 0.5, match, 0.0)
            wide = jnp.dot(chosen, spread, precision=HIGHEST, preferred_element_type=F32)
            wide = jnp.where(cell // count == lead, wide, 0.0)
            made.append(jnp.dot(turn, wide, precision=HIGHEST, preferred_element_type=F32))
        return made

    def remote(source, target, send, recv, p):
        return pltpu.make_async_remote_copy(src_ref=source, dst_ref=target, send_sem=send, recv_sem=recv,
                                            device_id=peer(p), device_id_type=MESH)

    pair = devices // 2

    def block(ref, p):
        return ref.at[pl.ds(p * count, count), :]

    def groups(ref, q):
        return ref.at[pl.ds(q * group, group), :]

    def pair_sum(q):
        return remote(groups(share, fars + q), groups(pair_in, q), psend.at[q], precv.at[q], pair)

    def chip_sum(p):
        return remote(block(share, p), block(chip_in, p), csend.at[p], crecv.at[p], p)

    def chip_gather(p):
        return remote(block(gathered, 0), block(gathered, p), gcsend.at[p], gcrecv.at[p], p)

    def pair_gather(q):
        return remote(groups(gathered, q), groups(gathered, fars + q), gpsend.at[q], gprecv.at[q], pair)

    for q in reversed(range(fars)):
        pick(half + q * group, group)
        pair_sum(q).start()
    for q in reversed(range(fars)):
        pick(q * group, group)
        pair_sum(q).wait_recv()
        at = slice(q * group, (q + 1) * group)
        share[at, :] = share[at, :] + pair_in[at, :]
        for p in reversed(range(max(q * mids, 1), (q + 1) * mids)):
            chip_sum(p).start()
    tables = sketch_tables()
    kept = share[0:count, :]
    for p in range(1, chips):
        chip_sum(p).wait_recv()
        kept = kept + chip_in[p * count:(p + 1) * count, :]
    gathered[0:count, :] = kept * (1.0 / math.sqrt(rows * devices))
    for p in reversed(range(1, chips)):
        chip_gather(p).start()

    def product(first, size):
        top, mid, low = three(gathered[first:first + size, :])
        left = jnp.concatenate([top, top, mid, top, low, mid], axis=0)
        right = jnp.concatenate([top, mid, top, low, top, mid], axis=0)
        return lax.dot_general(left, right, (((0,), (0,)), ((), ())), preferred_element_type=F32)

    gram = 0.0
    for q in range(fars):
        for p in range(max(q * mids, 1), (q + 1) * mids):
            chip_gather(p).wait_recv()
        pair_gather(q).start()
        gram = gram + product(q * group, group)

    rows_here = jnp.concatenate([gathered[q * group:q * group + 2 * count, :] for q in range(fars)], axis=0)
    top, mid, low = three(rows_here)
    table = jnp.concatenate(tables, axis=0).astype(BF16)
    picked = jnp.dot(jnp.concatenate([table, table, table], axis=1), jnp.concatenate([top, mid, low], axis=0),
                     preferred_element_type=F32)
    for m in range(MOST):
        sketch_ref[m, :, :] = picked[m * nl:(m + 1) * nl, :]
    for q in range(fars):
        pair_gather(q).wait_recv()
        gram = gram + product(half + q * group, group)
    gram_ref[...] = gram * (1.0 / total)

    for p in range(1, devices):
        note(p).wait_send()
    for q in range(fars):
        pair_sum(q).wait_send()
        pair_gather(q).wait_send()
    for p in range(1, chips):
        chip_sum(p).wait_send()
        chip_gather(p).wait_send()


def eliminate(both, hook):
    nb = both.shape[0]
    sub = lax.broadcasted_iota(jnp.int32, (8, both.shape[1]), 0)
    wide = (8, both.shape[1])
    tiles = [both[8 * g:8 * g + 8, :] for g in range(nb // 8)]
    for g0 in range(nb // 8):
        hook()
        cols = {}
        for g in range(g0, nb // 8):
            cols[g] = [jnp.broadcast_to(tiles[g][:, 8 * g0 + j:8 * g0 + j + 1], wide) for j in range(8)]
        for i in range(8):
            if i == 7 and g0 == nb // 8 - 1:
                break
            lead = cols[g0]
            flip = 1.0 / lead[i][i:i + 1, :]
            pivot = tiles[g0][i:i + 1, :]
            heads = [lead[j][i:i + 1, :] for j in range(8)]
            for g in range(g0, nb // 8):
                if g == g0 and i == 7:
                    continue
                rate = cols[g][i] * flip
                if g == g0:
                    rate = jnp.where(sub > i, rate, 0.0)
                for j in range(i + 1, 8):
                    cols[g][j] = cols[g][j] - rate * heads[j]
                tiles[g] = tiles[g] - rate * pivot
    return jnp.concatenate(tiles, axis=0)


def three(value):
    top = value.astype(BF16)
    value = value - top.astype(F32)
    mid = value.astype(BF16)
    return top, mid, (value - mid.astype(F32)).astype(BF16)


def factor_kernel(gram_ref, sketch_in, current_ref, sketch_ref, r_ref, out_ref,
                  xbuf, parts, obuf, load_sem, store_sem):
    rows, width = current_ref.shape
    blocks = width // BLOCK
    turns = width // 32
    pieces = turns
    step = rows // pieces
    wide = width // 2

    def load(c):
        at = pl.ds(c * step, step)
        return pltpu.make_async_copy(current_ref.at[at, :], xbuf.at[at, :], load_sem.at[c])

    def store(c, side):
        at = (pl.ds(c * step, step), pl.ds(side * wide, wide))
        return pltpu.make_async_copy(obuf.at[at], out_ref.at[at], store_sem.at[c, side])

    for c in range(pieces):
        load(c).start()
    for source in range(sketch_ref.shape[0]):
        for m in range(MOST):
            sketch_ref[source, m:m + 1, :] = sketch_in[m, source:source + 1, :]

    def split(c):
        load(c).wait()
        at = slice(c * step, (c + 1) * step)
        x = xbuf[at, :]
        top = x.astype(BF16)
        rest = (x - top.astype(F32)).astype(BF16)
        parts[at, 0:wide] = top[:, 0:wide]
        parts[at, wide:2 * wide] = rest[:, 0:wide]
        parts[at, 2 * wide:3 * wide] = top[:, wide:]
        parts[at, 3 * wide:] = rest[:, wide:]

    def turned(inverse):
        inverse = inverse.T
        top = inverse.astype(BF16)
        rest = (inverse - top.astype(F32)).astype(BF16)
        both = jnp.concatenate([top, rest], axis=1)
        return jnp.concatenate([both[k * wide:(k + 1) * wide, :]
                                for k in range(both.shape[0] // wide) for _ in range(2)], axis=0)

    def solve(first, last, stack, side):
        x = parts[first:last, 0:stack.shape[0]]
        both = jnp.dot(x, stack, preferred_element_type=F32)
        obuf[first:last, side * wide:(side + 1) * wide] = both[:, 0:wide] + both[:, wide:]

    state = {"turn": 0, "stack": None}

    def hook():
        turn = state["turn"]
        state["turn"] += 1
        if turns <= turn < 2 * turns:
            split(turn - turns)
        elif turn >= 2 * turns:
            turn -= 2 * turns
            half = step // 2
            solve(turn * half, (turn + 1) * half, state["stack"], 0)
            if turn % 2:
                store(turn // 2, 0).start()

    size = (BLOCK, LANES)
    row = lax.broadcasted_iota(jnp.int32, size, 0)
    lane = lax.broadcasted_iota(jnp.int32, size, 1)
    halves = range(width // LANES)
    left_half = lane < BLOCK
    unit = jnp.where(row == lane - BLOCK, 1.0, 0.0).astype(F32)
    a = [[gram_ref[k * BLOCK:(k + 1) * BLOCK, h * LANES:(h + 1) * LANES] for h in halves] for k in range(blocks)]
    inverse = []
    for k in range(blocks):
        first, last = k * BLOCK, (k + 1) * BLOCK
        if k == blocks // 2:
            state["stack"] = turned(jnp.concatenate(inverse, axis=0)[:, 0:wide])
        home, start = first // LANES, first % LANES
        own = a[k][home]
        if start:
            own = pltpu.roll(own, BLOCK, 1)
        both = eliminate(jnp.where(left_half, own, unit), hook)
        diag = jnp.sum(jnp.where(row == lane, both, 0.0), axis=1, keepdims=True)
        both = both * (1.0 / jnp.sqrt(diag))
        both = jnp.where(left_half, pltpu.roll(both, BLOCK, 1), both)
        top, mid, low = [part.astype(F32) for part in three(both)]
        left = jnp.concatenate([top, jnp.where(left_half, top, mid), jnp.where(left_half, mid, low)], axis=1).astype(BF16)
        top, mid, low = three(jnp.concatenate(a[k], axis=1))
        right = jnp.concatenate([top, mid, low, top, mid, top], axis=0)
        done = jnp.dot(left, right, preferred_element_type=F32)
        done = [done[:, h * LANES:(h + 1) * LANES] for h in halves]
        for h in halves:
            r_ref[first:last, h * LANES:(h + 1) * LANES] = jnp.where(row + first <= lane + h * LANES, done[h], 0.0)
        inside = (lane >= start) & (lane < start + BLOCK)
        done[home] = jnp.where(inside, both, done[home])
        inverse.append(jnp.concatenate([jnp.where(lane + h * LANES < last, done[h], 0.0) for h in halves], axis=1))
        if k == blocks - 1:
            break
        top, mid, low = three(jnp.concatenate(done, axis=1))
        base = last // LANES * LANES
        left = jnp.concatenate([top, top, mid, top, low, mid], axis=0)
        right = jnp.concatenate([top, mid, top, low, top, mid], axis=0)
        for part in range(base, width, LANES):
            change = lax.dot_general(left[:, part:part + LANES], right, (((0,), (0,)), ((), ())),
                                     preferred_element_type=F32)
            for later in range(max(k + 1, part // BLOCK), (part + LANES) // BLOCK):
                at = later * BLOCK - part
                for h in halves:
                    old = jnp.where(inside, 0.0, a[later][h]) if h == home else a[later][h]
                    a[later][h] = old - change[at:at + BLOCK, h * LANES:(h + 1) * LANES]
    stack = turned(jnp.concatenate(inverse[blocks // 2:], axis=0))
    for c in range(pieces):
        solve(c * step, (c + 1) * step, stack, 1)
        store(c, 1).start()
    for c in range(pieces):
        store(c, 0).wait()
        store(c, 1).wait()


def shards(nh, nl, current, signs, sample_rows, sample_owner):
    rows, width = current.shape
    count = sample_rows.shape[0]
    devices = nh * nl
    total = devices * count
    vmem = pl.BlockSpec(memory_space=pltpu.VMEM)
    anywhere = pl.BlockSpec(memory_space=pl.ANY)
    dma = pltpu.SemaphoreType.DMA
    gram, picked = pl.pallas_call(
        functools.partial(mix_kernel, nh, nl, count),
        name="mix",
        out_shape=(jax.ShapeDtypeStruct((width, width), F32),
                   jax.ShapeDtypeStruct((MOST, nl, width), F32)),
        in_specs=[anywhere, anywhere, anywhere, anywhere],
        out_specs=(vmem, vmem),
        scratch_shapes=[
            pltpu.VMEM((1, count), jnp.int32),
            pltpu.VMEM((1, count), jnp.int32),
            pltpu.VMEM((rows // LANES, LANES), jnp.int32),
            pltpu.VMEM((1, LANES), jnp.int32),
            pltpu.VMEM((devices, LANES), jnp.int32),
            pltpu.SMEM((devices, LANES), jnp.int32),
            pltpu.VMEM((rows, width), F32),
            pltpu.VMEM((rows, width), F32),
            pltpu.VMEM((total, width), F32),
            pltpu.VMEM((total // 2, width), F32),
            pltpu.VMEM((total // 2, width), F32),
            pltpu.VMEM((total, width), F32),
            dma((3,)), dma((rows // TILE,)), dma, dma((devices,)), dma((devices,)),
            dma((nl // 2,)), dma((nl // 2,)), dma((devices // 2,)), dma((devices // 2,)),
            dma((devices // 2,)), dma((devices // 2,)), dma((nl // 2,)), dma((nl // 2,)),
        ],
        compiler_params=pltpu.CompilerParams(
            collective_id=0, has_side_effects=True, vmem_limit_bytes=VMEM_LIMIT),
    )(sample_rows.reshape(1, count), sample_owner.reshape(1, count), signs.reshape(rows // LANES, LANES), current)
    sketch, r_factor, precond = pl.pallas_call(
        factor_kernel,
        name="factor",
        out_shape=(jax.ShapeDtypeStruct((nl, MOST, width), F32),
                   jax.ShapeDtypeStruct((width, width), F32),
                   jax.ShapeDtypeStruct((rows, width), F32)),
        in_specs=[vmem, vmem, anywhere],
        out_specs=(vmem, vmem, anywhere),
        scratch_shapes=[
            pltpu.VMEM((rows, width), F32),
            pltpu.VMEM((rows, 2 * width), BF16),
            pltpu.VMEM((rows, width), F32),
            dma((width // 32,)), dma((width // 32, 2)),
        ],
        compiler_params=pltpu.CompilerParams(vmem_limit_bytes=VMEM_LIMIT),
    )(gram, picked, current)
    return (sketch.reshape(1, 1, nl, MOST, width), r_factor, precond)


def solution(mesh):
    placed = (P(("hi", "lo"), None), P(("hi", "lo")), P(("hi", "lo")), P(("hi", "lo"), None))
    return jax.shard_map(
        functools.partial(shards, mesh.shape["hi"], mesh.shape["lo"]),
        mesh=mesh,
        in_specs=placed,
        out_specs=(P("hi", "lo", None, None, None), P(), P(("hi", "lo"), None)),
        check_vma=False,
    )
```
